32 devices in a mesh: tx: 4 (over y, x), ty: 2 (over core), depth: 4 (over z).
Axes of the slice: x: 2, y: 2, z: 4, core: 2. Of those that a mesh axis runs over, the one named last changes fastest.
Arguments:
- volume: bfloat16 [128, 512, 512], P('depth', 'ty', 'tx'), may hold values from -6 to 6
- transfer: float32 [4, 2], replicated, may hold values from -1.5 to 1.5
- ray_start: int32 [4, 512, 512], P('depth', 'ty', 'tx'), may hold values from 0 to 15
- ray_stop: int32 [4, 512, 512], P('depth', 'ty', 'tx'), may hold values from 16 to 32
- pattern: int32 [4, 64, 4], P('depth', 'ty', 'tx'), may hold values 0 or 1
- depth_order: int32 [4], replicated, may hold values from 0 to 3, each once
Outputs:
- frame: float32 [4, 512, 512], P(None, 'ty', 'tx')
The draws below stay inside these ranges and needn't reach their ends.
Inputs may be any that keep to these rules, and one draw needn't show every extreme that they name: ray_start[s] < ray_stop[s] for every ray and slice. `depth_order`: each slice appears once.
All inputs are finite; a program needn't handle non-finite values. No bound on the sum of `pattern` on one device may be relied on, other than what follows from the above.
Results may differ from the reference program's by a relative error of at most 0.0003.
Values may be sent and summed in bfloat16 or wider, within the bound.
A program may use at most 64 MiB of HBM per device.

```python
import jax
import jax.numpy as jnp
from jax import lax

BZ = 32
NZ = 128
NY = 512
NX = 512
N_DEPTH = 4


def set_ends(result, key, least, top_value):
    spot = [jax.random.randint(jax.random.fold_in(key, axis), (), 0, length) for axis, length in enumerate(result.shape)]
    widest = result.shape.index(max(result.shape))
    neighbour = spot[:widest] + [(spot[widest] + 1) % result.shape[widest]] + spot[widest + 1:]
    return result.at[tuple(spot)].set(least).at[tuple(neighbour)].set(top_value)


def shard_levels(stream_key, shape, split, smallest, largest):
    loudness = 1.0
    for dim, shards_of in split:
        steps = jax.random.uniform(jax.random.fold_in(jax.random.fold_in(stream_key, 6), dim), (shards_of,), jnp.float32, smallest / len(split), largest / len(split))
        loudness = loudness * jnp.repeat(jnp.exp(steps), shape[dim] // shards_of).reshape((-1,) + (1,) * (len(shape) - 1 - dim))
    return loudness


def scatter_about(key, shape, scale, reach, split=(), kind=jnp.bfloat16):
    loudness = shard_levels(key, shape, split, -0.22, 0.18) if split else 1.0
    values = jax.random.normal(key, shape, jnp.float32) * scale * loudness
    return jnp.minimum(jnp.maximum(values, -reach), reach).astype(kind)


def setup_inputs(seed: int = 0) -> dict:
    splits = jax.random.split(jax.random.key(seed), 7)
    return {
        "volume": scatter_about(splits[0], (NZ, NY, NX), 1.0, 6.0, ((0, 4), (1, 2), (2, 4))),
        "transfer": jnp.clip(jax.random.uniform(splits[1], (4, 2), jnp.float32, -1.5, 1.5), -1.5, 1.5),
        "ray_start": set_ends(jax.random.randint(splits[2], (N_DEPTH, NY, NX), 0, BZ // 2), jax.random.fold_in(splits[2], 1), 0, (BZ // 2) - 1).astype(jnp.int32),
        "ray_stop": set_ends(jax.random.randint(splits[3], (N_DEPTH, NY, NX), BZ // 2, BZ + 1), jax.random.fold_in(splits[3], 1), BZ // 2, BZ).astype(jnp.int32),
        "pattern": set_ends((jax.random.randint(splits[4], (N_DEPTH, NY // 8, NX // 128), 0, 4) < 3).astype(jnp.int32), jax.random.fold_in(splits[4], 1), 0, 1),
        "depth_order": jax.random.permutation(splits[5], N_DEPTH).astype(jnp.int32),
    }


def local_partial(padded, transfer, ray_start, ray_stop, pattern, depth_count):
    samples = padded.shape[0] - 2
    values = padded[1:-1, 1:-1, 1:-1]
    grad_z = (padded[2:, 1:-1, 1:-1] - padded[:-2, 1:-1, 1:-1]) * 0.5
    grad_y = (padded[1:-1, 2:, 1:-1] - padded[1:-1, :-2, 1:-1]) * 0.5
    grad_x = (padded[1:-1, 1:-1, 2:] - padded[1:-1, 1:-1, :-2]) * 0.5
    lit = jnp.abs(0.48 * grad_x + 0.6 * grad_y + 0.64 * grad_z)
    shading = 0.3 + 0.7 * lit / jnp.sqrt(grad_x * grad_x + grad_y * grad_y + grad_z * grad_z + 1.0)
    rows_each = ray_start.shape[0] // pattern.shape[0]
    cols_each = ray_start.shape[1] // pattern.shape[1]
    pattern_full = jnp.repeat(jnp.repeat(pattern, rows_each, axis=0), cols_each, axis=1)
    layers = lax.broadcasted_iota(jnp.int32, (samples, 1, 1), 0)
    active = (layers >= ray_start[None]) & (layers < ray_stop[None]) & (pattern_full[None] > 0)
    density = jax.nn.softplus(transfer[3, 0] * values + transfer[3, 1]) * (2.0 / (samples * depth_count))
    opacity = jnp.where(active, 1.0 - jnp.exp(-density), jnp.float32(0.0))
    passed = jnp.cumprod(1.0 - opacity, axis=0)
    prior = jnp.concatenate([jnp.ones_like(passed[:1]), passed[:-1]], axis=0)
    weights = prior * opacity * shading
    tinted = jax.nn.sigmoid(transfer[:3, 0][:, None, None, None] * values[None] + transfer[:3, 1][:, None, None, None])
    colors = lax.optimization_barrier(jnp.sum(weights[None] * tinted, axis=1))
    return jnp.concatenate([colors, passed[-1][None]], axis=0)

def composite(partials, depth_order):
    count = partials.shape[0]

    def step(position, state_pair):
        colors, remain = state_pair
        slice_part = lax.dynamic_index_in_dim(partials, depth_order[position], 0, keepdims=False)
        return (colors + remain[None] * slice_part[:3], remain * slice_part[3])
    start_pair = (jnp.zeros(partials.shape[1:2 - 1 + 1][:0] + (3,) + partials.shape[2:], jnp.float32), jnp.ones(partials.shape[2:], jnp.float32))
    colors, remain = lax.fori_loop(0, count, step, start_pair)
    return jnp.concatenate([colors, 1.0 - remain[None]], axis=0)

def reference(volume, transfer, ray_start, ray_stop, pattern, depth_order):
    padz = jnp.pad(volume, ((1, 1), (0, 0), (0, 0)))

    def one_slice(slice_index):
        bricks = lax.dynamic_slice_in_dim(padz, slice_index * BZ, BZ + 2, 0).astype(jnp.float32)
        bricks = jnp.pad(bricks, ((0, 0), (1, 1), (1, 1)))
        return local_partial(bricks, transfer, ray_start[slice_index], ray_stop[slice_index], pattern[slice_index], N_DEPTH)
    partials = lax.map(one_slice, jnp.arange(N_DEPTH, dtype=jnp.int32))
    return composite(partials, depth_order)
```

```python
import functools
import math

import jax
import jax.numpy as jnp
from jax import lax
from jax.experimental import pallas as pl
from jax.experimental.pallas import tpu as pltpu
from jax.sharding import PartitionSpec as P

MESH = pl.DeviceIdType.MESH
STRIP = 16
UNROLL = 32
LOG2E = math.log2(math.e)
OCTAVES = 24
CODES = 65535.0 / OCTAVES
LEVELS = 65000.0
MERGE_LAG = 4
RELAY_LAG = 7
HIDE_LAG = 3


def encode(x):
    place = jnp.log(jnp.clip(x, 1e-30, 1.0)) * (CODES * LOG2E) + 65535.5
    return (jnp.maximum(place, 0.0).astype(jnp.int32) - 32768).astype(jnp.int16)


def decode(code):
    wide = code.astype(jnp.int32)
    value = jnp.exp2((wide.astype(jnp.float32) - 32767.0) * (1.0 / CODES))
    return jnp.where(wide == -32768, 0.0, value)


def to_level(x):
    return (jnp.minimum(x + 0.5, 65535.0).astype(jnp.int32) - 32768).astype(jnp.int16)


def from_level(code):
    return code.astype(jnp.int32).astype(jnp.float32) + 32768.0


def kernel(
    n, n_tx, n_ty, scale, each,
    vol, start_hbm, stop_hbm, pattern, transfer, order, out,
    vb, start, stop, yup, ydn, edge, xl, xr, vf, share,
    hide, hides, part, parts, factor,
    load_sem, halo_send, halo_recv, edge_send, edge_recv, far,
    hide_send, hide_recv, part_send, part_recv, fin_send, fin_recv, top_send, top_recv,
):
    samples, ny, nx = vol.shape
    chunks = ny // each
    group = 2 * each
    last_chunk = chunks - 1
    second = last_chunk // 2
    slots = last_chunk - second + 1
    tx, ty, me = lax.axis_index("tx"), lax.axis_index("ty"), lax.axis_index("depth")

    def rows_of(j):
        return pl.ds(pl.multiple_of(j * each, each), each)

    def owner_of(j):
        return jnp.where(j < second, n // 2, n // 2 - 1)

    def slot_of(j):
        return jnp.where(j < second, j, jnp.where(j == last_chunk, slots - 1, j - second))

    def load_piece(j):
        return pltpu.make_async_copy(
            vol.at[:, rows_of(j)], vb.at[pl.ds(1, samples), rows_of(j)], load_sem.at[j]
        )

    loads = [
        pltpu.make_async_copy(start_hbm.at[0], start, load_sem.at[chunks]),
        pltpu.make_async_copy(stop_hbm.at[0], stop, load_sem.at[chunks + 1]),
    ]
    barrier = pltpu.get_barrier_semaphore()
    sides = (("tx", tx, n_tx), ("ty", ty, n_ty), ("depth", me, n))
    expected = 0
    for axis, at, count in sides:
        @pl.when(at > 0)
        def _(axis=axis, at=at):
            pl.semaphore_signal(barrier, inc=1, device_id={axis: at - 1}, device_id_type=MESH)

        @pl.when(at < count - 1)
        def _(axis=axis, at=at):
            pl.semaphore_signal(barrier, inc=1, device_id={axis: at + 1}, device_id_type=MESH)

        expected = expected + jnp.where(at > 0, 1, 0) + jnp.where(at < count - 1, 1, 0)

    load_piece(0).start()
    for load in loads:
        load.start()
    for j in range(1, chunks):
        load_piece(j).start()
    pl.semaphore_wait(barrier, expected)

    def far_signal(r):
        @pl.when((me - r + 1 >= 0) & (me + 1 < n))
        def _():
            pl.semaphore_signal(far.at[r, 0], inc=1, device_id={"depth": me + 1}, device_id_type=MESH)

        @pl.when((me + r - 1 < n) & (me - 1 >= 0))
        def _():
            pl.semaphore_signal(far.at[r, 1], inc=1, device_id={"depth": me - 1}, device_id_type=MESH)

    def far_wait(r):
        @pl.when(me - r >= 0)
        def _():
            pl.semaphore_wait(far.at[r, 0], 1)

        @pl.when(me + r < n)
        def _():
            pl.semaphore_wait(far.at[r, 1], 1)

        if r + 1 < n:
            far_signal(r + 1)

    def shift(sems, slot, axis, at, source, target, upward):
        return pltpu.make_async_remote_copy(
            src_ref=source, dst_ref=target, send_sem=sems[0].at[slot], recv_sem=sems[1].at[slot],
            device_id={axis: at + 1 if upward else at - 1}, device_id_type=MESH,
        )

    halo = (halo_send, halo_recv)
    last, first = pl.ds(ny - STRIP, STRIP), pl.ds(0, STRIP)
    halos = [
        (shift(halo, 2, "ty", ty, vol.at[:, last], yup, True), ty, n_ty, True, lambda: yup),
        (shift(halo, 3, "ty", ty, vol.at[:, first], ydn, False), ty, n_ty, False, lambda: ydn),
        (shift(halo, 0, "depth", me, vol.at[samples - 1], vb.at[0], True), me, n, True, lambda: vb.at[0]),
        (shift(halo, 1, "depth", me, vol.at[0], vb.at[samples + 1], False), me, n, False, lambda: vb.at[samples + 1]),
    ]

    def edge_copies(g):
        rows = pl.ds(pl.multiple_of(g * group, group), group)
        sems = (edge_send, edge_recv)
        return [
            (shift(sems, 2 * g, "tx", tx, edge.at[rows], xl.at[rows], True), tx, n_tx, True, None),
            (shift(sems, 2 * g + 1, "tx", tx, edge.at[rows], xr.at[rows], False), tx, n_tx, False, None),
        ]

    def send_halo(entry):
        copy, at, count, upward, place = entry
        pl.when(at < count - 1 if upward else at > 0)(copy.start)
        if place is not None:
            @pl.when(at == 0 if upward else at == count - 1)
            def _():
                place()[...] = jnp.zeros(place().shape, jnp.bfloat16)

    def wait_sent(entry):
        copy, at, count, upward, _ = entry
        pl.when(at < count - 1 if upward else at > 0)(copy.wait_send)

    def wait_arrived(entry):
        copy, at, count, upward, _ = entry
        pl.when(at > 0 if upward else at < count - 1)(copy.wait_recv)

    for entry in halos:
        send_halo(entry)
    if n > 2:
        far_signal(2)

    for at, count, place in ((tx, 0, xl), (tx, n_tx - 1, xr)):
        @pl.when(at == count)
        def _(place=place):
            place[...] = jnp.zeros(place.shape, jnp.bfloat16)

    rows_each = ny // pattern.shape[1]
    slopes = [transfer[0, i] * 0.5 for i in range(3)]
    offsets = [transfer[1, i] * 0.5 for i in range(3)]
    slope, offset = transfer[0, 3] * LOG2E, transfer[1, 3] * LOG2E

    rank = [sum(jnp.where(order[q] == s, q, 0) for q in range(n)) for s in range(n)]
    before = [[jnp.where(rank[a] < rank[b], 1.0, 0.0) for b in range(n)] for a in range(n)]
    lane = lax.broadcasted_iota(jnp.int32, (each, nx), 1)
    pair = lax.shift_right_arithmetic(lane, 1)

    for load in loads:
        load.wait()

    @pl.loop(0, chunks)
    def _(j):
        load_piece(j).wait()
        r0 = pl.multiple_of(j * each, each)
        rows, inner = rows_of(j), pl.ds(pl.multiple_of(r0 + 8, 8), each)
        begins, ends = [], []
        for b in range(each // rows_each):
            on = pattern[0, j * (each // rows_each) + b] > 0
            block = pl.ds(pl.multiple_of(r0 + b * rows_each, rows_each), rows_each)
            begins.append(jnp.where(on, start[block], samples))
            ends.append(jnp.where(on, stop[block], 0))
        begin, end = jnp.concatenate(begins, axis=0), jnp.concatenate(ends, axis=0)

        def layer(early, z, state):
            passed, edges = state
            v = vb[z + 1, rows].astype(jnp.float32)
            vf[z + 1, inner] = v
            edges = jnp.where(pair == z, pltpu.roll(v, lax.rem(2 * z + 1, nx), 1), edges)
            log = jnp.log(1.0 + jnp.exp2(v * slope + offset))
            through = jnp.exp2(log * (-scale * LOG2E))
            now = jnp.where(begin <= z if early else end > z, passed * through, passed)
            share[z, rows] = passed - now
            return now, edges

        state = (jnp.ones((each, nx), jnp.float32), jnp.zeros((each, nx), jnp.float32))
        state = lax.fori_loop(0, samples // 2, functools.partial(layer, True), state, unroll=UNROLL // 2)
        passed, edges = lax.fori_loop(samples // 2, samples, functools.partial(layer, False), state, unroll=UNROLL // 2)
        edge[rows] = edges.astype(jnp.bfloat16)
        hide[j] = encode(1.0 - passed)

        @pl.when(lax.rem(j, 2) == 1)
        def _():
            for entry in edge_copies(j // 2):
                send_halo(entry)

    def to_merger(source, target, sends, recvs, j, dest):
        return pltpu.make_async_remote_copy(
            src_ref=source.at[j], dst_ref=target.at[me, slot_of(j)],
            send_sem=sends.at[j, lax.rem(dest + n - me, n)], recv_sem=recvs.at[me, slot_of(j)],
            device_id={"depth": dest}, device_id_type=MESH,
        )

    def hide_copy(j, dest):
        return to_merger(hide, hides, hide_send, hide_recv, j, dest)

    def part_copy(j, dest):
        return to_merger(part, parts, part_send, part_recv, j, dest)

    def wait_from(source, target, sends, recvs, j):
        for rel in range(1, n):
            other = lax.rem(me + rel, n)
            pltpu.make_async_remote_copy(
                src_ref=source.at[j], dst_ref=target.at[other, slot_of(j)],
                send_sem=sends.at[j, rel], recv_sem=recvs.at[other, slot_of(j)],
                device_id={"depth": other}, device_id_type=MESH,
            ).wait_recv()

    def send_to_merger(copy, source, target, j):
        owner = owner_of(j)

        @pl.when(owner == me)
        def _():
            target[me, slot_of(j)] = source[j]

        @pl.when(owner != me)
        def _():
            copy(j, owner).start()

    def send_to_all(copy, source, target):
        target[me, slots - 1] = source[last_chunk]
        for rel in range(1, n):
            copy(last_chunk, lax.rem(me + rel, n)).start()

    def top_copy(j, right):
        return pltpu.make_async_remote_copy(
            src_ref=out.at[3, rows_of(j)], dst_ref=out.at[3, rows_of(j)],
            send_sem=top_send.at[j, 1 if right else 0], recv_sem=top_recv.at[j],
            device_id={"depth": me + 1 if right else me - 1}, device_id_type=MESH,
        )

    def fin_copy(j, right):
        return pltpu.make_async_remote_copy(
            src_ref=out.at[pl.ds(0, 3), rows_of(j)], dst_ref=out.at[pl.ds(0, 3), rows_of(j)],
            send_sem=fin_send.at[j, 1 if right else 0], recv_sem=fin_recv.at[j],
            device_id={"depth": me + 1 if right else me - 1}, device_id_type=MESH,
        )

    def spread(copy, j, act):
        owner = owner_of(j)
        pl.when((me >= owner) & (me < n - 1))(lambda: act(copy(j, True)))
        pl.when((me <= owner) & (me > 0))(lambda: act(copy(j, False)))

    def relay(copy, j):
        @pl.when(owner_of(j) != me)
        def _():
            copy(j, True).wait_recv()
            spread(copy, j, lambda c: c.start())

    for r in range(2, max(3, n // 2 + 1)):
        if r < n:
            far_wait(r)

    @pl.loop(0, last_chunk)
    def _(j):
        send_to_merger(hide_copy, hide, hides, j)

    for entry in halos:
        wait_arrived(entry)

    @pl.loop(0, samples, unroll=4)
    def _(z):
        vf[1 + z, pl.ds(0, 8)] = yup[z].astype(jnp.float32)[STRIP - 8:]
        vf[1 + z, pl.ds(8 + ny, 8)] = ydn[z].astype(jnp.float32)[:8]

    def render(j):
        r0 = pl.multiple_of(j * each, each)
        rows, inner = rows_of(j), pl.ds(pl.multiple_of(r0 + 8, 8), each)

        @pl.when(lax.rem(j, 2) == 0)
        def _():
            for entry in edge_copies(j // 2):
                wait_arrived(entry)

        vf[samples + 1, inner] = vb[samples + 1, rows].astype(jnp.float32)
        beyond = pltpu.roll(xr[rows].astype(jnp.float32), nx - 2, 1)
        sides_of = jnp.where(lax.rem(lane, 2) == 0, xl[rows].astype(jnp.float32), beyond)

        def layer(z, state):
            previous, v, total, red, green, blue = state
            after = vf[z + 2, inner]
            near = vf.at[z + 1, pl.ds(r0, each + 16)]
            dz = after - previous
            dyv = near[pl.ds(9, each)] - near[pl.ds(7, each)]
            beside = pltpu.roll(sides_of, lax.rem(nx - 2 * z, nx), 1)
            right = jnp.where(lane == nx - 1, beside, pltpu.roll(v, nx - 1, 1))
            dxv = right - jnp.where(lane == 0, beside, pltpu.roll(v, 1, 1))
            lit = jnp.abs(dxv + 1.25 * dyv + (0.224 / 0.168) * dz)
            shade = (0.15 / 0.168) + lit * lax.rsqrt(dxv * dxv + dyv * dyv + dz * dz + 4.0)
            weight = share[z, rows] * shade
            tints = [jnp.tanh(v * slopes[i] + offsets[i]) for i in range(3)]
            return (
                v, after, total + weight,
                red + weight * tints[0], green + weight * tints[1], blue + weight * tints[2],
            )

        zero = jnp.zeros((each, nx), jnp.float32)
        state = (vb[0, rows].astype(jnp.float32), vf[1, inner], zero, zero, zero, zero)
        _, _, total, red, green, blue = lax.fori_loop(0, samples, layer, state, unroll=UNROLL)
        per = (LEVELS * 0.168) / jnp.maximum(decode(hide[j]), 1e-30)
        for i, value in enumerate((red, green, blue)):
            part[j, i] = to_level((value + total) * per)

    def veil(j):
        slot = slot_of(j)
        wait_from(hide, hides, hide_send, hide_recv, j)
        hidden = [decode(hides[s, slot]) for s in range(n)]
        top = hidden[0]
        for s in range(1, n):
            top = top + hidden[s] * (1.0 - top)
        code = encode(top)
        out[3, rows_of(j)] = code
        per = 1.0 / jnp.maximum(decode(code), 1e-30)
        for s in range(n):
            weight = hidden[s] * per
            for a in range(n):
                if a != s:
                    weight = weight * (1.0 - hidden[a] * before[a][s])
            factor[slot, s] = weight

    def merge(j):
        slot = slot_of(j)
        wait_from(part, parts, part_send, part_recv, j)
        for i in range(3):
            level = from_level(parts[0, slot, i]) * factor[slot, 0]
            for s in range(1, n):
                level = level + from_level(parts[s, slot, i]) * factor[slot, s]
            out[i, rows_of(j)] = to_level(level)

    def owned(j, act):
        pl.when((j >= 0) & (j < last_chunk) & (owner_of(j) == me))(act)

    def veil_owned(j):
        veil(j)
        spread(top_copy, j, lambda c: c.start())

    def merge_owned(j):
        merge(j)
        spread(fin_copy, j, lambda c: c.start())

    @pl.loop(0, last_chunk + RELAY_LAG)
    def _(i):
        @pl.when(i < chunks)
        def _():
            render(i)

            @pl.when(i == 0)
            def _():
                for r in range(max(3, n // 2 + 1), n):
                    far_wait(r)
                send_to_all(hide_copy, hide, hides)

            pl.when(i < last_chunk)(lambda: send_to_merger(part_copy, part, parts, i))
            pl.when(i == last_chunk)(lambda: send_to_all(part_copy, part, parts))

        for offset in range(2):
            j = 2 * (i - HIDE_LAG) + offset
            owned(j, functools.partial(veil_owned, j))
        pl.when(i == last_chunk)(lambda: veil(last_chunk))
        owned(i - MERGE_LAG, lambda: merge_owned(i - MERGE_LAG))
        pl.when(i == last_chunk + MERGE_LAG)(lambda: merge(last_chunk))
        j = i - RELAY_LAG

        @pl.when((j >= 0) & (j < last_chunk))
        def _():
            relay(top_copy, j)
            relay(fin_copy, j)

    for entry in halos:
        wait_sent(entry)
    for g in range(chunks // 2):
        for entry in edge_copies(g):
            wait_sent(entry)

    @pl.loop(0, last_chunk)
    def _(j):
        @pl.when(owner_of(j) != me)
        def _():
            hide_copy(j, owner_of(j)).wait_send()
            part_copy(j, owner_of(j)).wait_send()

        spread(top_copy, j, lambda c: c.wait_send())
        spread(fin_copy, j, lambda c: c.wait_send())

    for rel in range(1, n):
        hide_copy(last_chunk, lax.rem(me + rel, n)).wait_send()
        part_copy(last_chunk, lax.rem(me + rel, n)).wait_send()


def solution(mesh):
    n, n_tx, n_ty = mesh.shape["depth"], mesh.shape["tx"], mesh.shape["ty"]

    def shards(volume, transfer, ray_start, ray_stop, pattern, depth_order):
        samples, ny, nx = volume.shape
        rows = min(32, ny // 4)
        chunks = ny // rows
        slots = chunks - 1 - (chunks - 1) // 2 + 1
        f32, bf16, i16 = jnp.float32, jnp.bfloat16, jnp.int16
        any_space = pl.BlockSpec(memory_space=pl.ANY)
        smem = pl.BlockSpec(memory_space=pltpu.SMEM)
        dma = pltpu.SemaphoreType.DMA
        codes = pl.pallas_call(
            functools.partial(kernel, n, n_tx, n_ty, 2.0 / (samples * n), rows),
            out_shape=jax.ShapeDtypeStruct((4, ny, nx), i16),
            in_specs=[any_space, any_space, any_space, smem, smem, smem],
            out_specs=pl.BlockSpec(memory_space=pltpu.VMEM),
            scratch_shapes=[
                pltpu.VMEM((samples + 2, ny, nx), bf16),
                pltpu.VMEM((ny, nx), jnp.int32),
                pltpu.VMEM((ny, nx), jnp.int32),
                pltpu.VMEM((samples, STRIP, nx), bf16),
                pltpu.VMEM((samples, STRIP, nx), bf16),
                pltpu.VMEM((ny, nx), bf16),
                pltpu.VMEM((ny, nx), bf16),
                pltpu.VMEM((ny, nx), bf16),
                pltpu.VMEM((samples + 2, ny + 16, nx), f32),
                pltpu.VMEM((samples, ny, nx), f32),
                pltpu.VMEM((chunks, rows, nx), i16),
                pltpu.VMEM((n, slots, rows, nx), i16),
                pltpu.VMEM((chunks, 3, rows, nx), i16),
                pltpu.VMEM((n, slots, 3, rows, nx), i16),
                pltpu.VMEM((slots, n, rows, nx), f32),
                dma((chunks + 2,)), dma((4,)), dma((4,)), dma((chunks,)), dma((chunks,)),
                pltpu.SemaphoreType.REGULAR((n, 2)),
                dma((chunks, n)), dma((n, slots)), dma((chunks, n)), dma((n, slots)),
                dma((chunks, 2)), dma((chunks,)), dma((chunks, 2)), dma((chunks,)),
            ],
            compiler_params=pltpu.CompilerParams(
                collective_id=0, has_side_effects=True, vmem_limit_bytes=62 * 1024 * 1024
            ),
        )(volume, ray_start, ray_stop, pattern[:, :, 0], transfer.T, depth_order)
        top = decode(codes[3])
        colors = from_level(codes[:3]) * (top * (1.0 / LEVELS))
        return jnp.concatenate([colors, top[None]], axis=0)

    in_specs = (
        P("depth", "ty", "tx"),
        P(),
        P("depth", "ty", "tx"),
        P("depth", "ty", "tx"),
        P("depth", "ty", "tx"),
        P(),
    )
    return jax.shard_map(shards, mesh=mesh, in_specs=in_specs, out_specs=P(None, "ty", "tx"), check_vma=False)
```

```python
import functools
import math

import jax
import jax.numpy as jnp
from jax import lax
from jax.experimental import pallas as pl
from jax.experimental.pallas import tpu as pltpu
from jax.sharding import PartitionSpec as P

MESH = pl.DeviceIdType.MESH
STRIP = 16
UNROLL = 32
LOG2E = math.log2(math.e)
OCTAVES = 24
CODES = 65535.0 / OCTAVES
LEVELS = 65000.0
VEIL_LAG = 4
MERGE_LAG = 6


def encode(x):
    place = jnp.log(jnp.clip(x, 1e-30, 1.0)) * (CODES * LOG2E) + 65535.5
    return (jnp.maximum(place, 0.0).astype(jnp.int32) - 32768).astype(jnp.int16)


def decode(code):
    wide = code.astype(jnp.int32)
    value = jnp.exp2((wide.astype(jnp.float32) - 32767.0) * (1.0 / CODES))
    return jnp.where(wide == -32768, 0.0, value)


def to_level(x):
    return (jnp.minimum(x + 0.5, 65535.0).astype(jnp.int32) - 32768).astype(jnp.int16)


def from_level(code):
    return code.astype(jnp.int32).astype(jnp.float32) + 32768.0


def kernel(
    n, n_tx, n_ty, scale, each,
    vol, start_hbm, stop_hbm, pattern, transfer, order, out,
    vb, start, stop, yup, ydn, edge, xl, xr, vf, share,
    hide, hides, part, parts, factor,
    load_sem, halo_send, halo_recv, deep_send, deep_recv, edge_send, edge_recv, far,
    hide_send, hide_recv, part_send, part_recv, fin_send, fin_recv, top_send, top_recv,
):
    samples, ny, nx = vol.shape
    chunks = ny // each
    group = 2 * each
    groups = chunks // 2
    mergers = (n // 2 - 1, n // 2)
    tx, ty, me = lax.axis_index("tx"), lax.axis_index("ty"), lax.axis_index("depth")

    def rows_of(j):
        return pl.ds(pl.multiple_of(j * each, each), each)

    def group_of(g):
        return pl.ds(pl.multiple_of(g * group, group), group)

    def load_piece(j):
        return pltpu.make_async_copy(
            vol.at[:, rows_of(j)], vb.at[pl.ds(1, samples), rows_of(j)], load_sem.at[j]
        )

    loads = [
        pltpu.make_async_copy(start_hbm.at[0], start, load_sem.at[chunks]),
        pltpu.make_async_copy(stop_hbm.at[0], stop, load_sem.at[chunks + 1]),
    ]
    barrier = pltpu.get_barrier_semaphore()
    sides = (("tx", tx, n_tx), ("ty", ty, n_ty), ("depth", me, n))
    expected = 0
    for axis, at, count in sides:
        @pl.when(at > 0)
        def _(axis=axis, at=at):
            pl.semaphore_signal(barrier, inc=1, device_id={axis: at - 1}, device_id_type=MESH)

        @pl.when(at < count - 1)
        def _(axis=axis, at=at):
            pl.semaphore_signal(barrier, inc=1, device_id={axis: at + 1}, device_id_type=MESH)

        expected = expected + jnp.where(at > 0, 1, 0) + jnp.where(at < count - 1, 1, 0)

    load_piece(0).start()
    for load in loads:
        load.start()
    for j in range(1, chunks):
        load_piece(j).start()
    pl.semaphore_wait(barrier, expected)

    def far_signal(r):
        @pl.when((me - r + 1 >= 0) & (me + 1 < n))
        def _():
            pl.semaphore_signal(far.at[r, 0], inc=1, device_id={"depth": me + 1}, device_id_type=MESH)

        @pl.when((me + r - 1 < n) & (me - 1 >= 0))
        def _():
            pl.semaphore_signal(far.at[r, 1], inc=1, device_id={"depth": me - 1}, device_id_type=MESH)

    def far_wait(r):
        @pl.when(me - r >= 0)
        def _():
            pl.semaphore_wait(far.at[r, 0], 1)

        @pl.when(me + r < n)
        def _():
            pl.semaphore_wait(far.at[r, 1], 1)

        if r + 1 < n:
            far_signal(r + 1)

    def shift(sems, slot, axis, at, source, target, upward):
        return pltpu.make_async_remote_copy(
            src_ref=source, dst_ref=target, send_sem=sems[0].at[slot], recv_sem=sems[1].at[slot],
            device_id={axis: at + 1 if upward else at - 1}, device_id_type=MESH,
        )

    halo = (halo_send, halo_recv)
    last, first = pl.ds(ny - STRIP, STRIP), pl.ds(0, STRIP)
    halos = [
        (shift(halo, 0, "ty", ty, vol.at[:, last], yup, True), ty, n_ty, True, lambda: yup),
        (shift(halo, 1, "ty", ty, vol.at[:, first], ydn, False), ty, n_ty, False, lambda: ydn),
    ]

    def deep_copies(g):
        rows = group_of(g)
        sems = (deep_send, deep_recv)
        return [
            (shift(sems, 2 * g, "depth", me, vol.at[samples - 1, rows], vb.at[0, rows], True), me, n, True, None),
            (shift(sems, 2 * g + 1, "depth", me, vol.at[0, rows], vb.at[samples + 1, rows], False), me, n, False, None),
        ]

    def edge_copies(g):
        rows = pl.ds(pl.multiple_of(g * group, group), group)
        sems = (edge_send, edge_recv)
        return [
            (shift(sems, 2 * g, "tx", tx, edge.at[rows], xl.at[rows], True), tx, n_tx, True, None),
            (shift(sems, 2 * g + 1, "tx", tx, edge.at[rows], xr.at[rows], False), tx, n_tx, False, None),
        ]

    def send_halo(entry):
        copy, at, count, upward, place = entry
        pl.when(at < count - 1 if upward else at > 0)(copy.start)
        if place is not None:
            @pl.when(at == 0 if upward else at == count - 1)
            def _():
                place()[...] = jnp.zeros(place().shape, jnp.bfloat16)

    def wait_sent(entry):
        copy, at, count, upward, _ = entry
        pl.when(at < count - 1 if upward else at > 0)(copy.wait_send)

    def wait_arrived(entry):
        copy, at, count, upward, _ = entry
        pl.when(at > 0 if upward else at < count - 1)(copy.wait_recv)

    for g in range(groups):
        for entry in deep_copies(g):
            send_halo(entry)
    for entry in halos:
        send_halo(entry)
    if n > 2:
        far_signal(2)

    for at, edge_at, place in (
        (tx, 0, xl), (tx, n_tx - 1, xr), (me, 0, vb.at[0]), (me, n - 1, vb.at[samples + 1]),
    ):
        @pl.when(at == edge_at)
        def _(place=place):
            place[...] = jnp.zeros(place.shape, jnp.bfloat16)

    rows_each = ny // pattern.shape[1]
    slopes = [transfer[0, i] * 0.5 for i in range(3)]
    offsets = [transfer[1, i] * 0.5 for i in range(3)]
    slope, offset = transfer[0, 3] * LOG2E, transfer[1, 3] * LOG2E

    rank = [sum(jnp.where(order[q] == s, q, 0) for q in range(n)) for s in range(n)]
    before = [[jnp.where(rank[a] < rank[b], 1.0, 0.0) for b in range(n)] for a in range(n)]
    lane = lax.broadcasted_iota(jnp.int32, (each, nx), 1)
    pair = lax.shift_right_arithmetic(lane, 1)

    merging = (me == mergers[0]) | (me == mergers[1])
    handing = (me > 0) & (me < n - 1)
    hide_refs = (hide, hides, hide_send, hide_recv, 2)
    part_refs = (part, parts, part_send, part_recv, 1)

    def to_merger(source, target, sends, recvs, count, j, origin, which):
        block = pl.ds(j * count, count)
        return pltpu.make_async_remote_copy(
            src_ref=source.at[block], dst_ref=target.at[origin, block],
            send_sem=sends.at[j, which], recv_sem=recvs.at[origin, j],
            device_id={"depth": mergers[which]}, device_id_type=MESH,
        )

    def send_to_mergers(refs, j):
        for which, merger in enumerate(mergers):
            pl.when(me != merger)(lambda: to_merger(*refs, j, me, which).start())

        @pl.when(merging)
        def _():
            for c in range(refs[4]):
                refs[1][me, j * refs[4] + c] = refs[0][j * refs[4] + c]

    def wait_parts(refs, j):
        for s in range(n):
            pl.when(me != s)(lambda: to_merger(*refs, j, s, 0).wait_recv())

    def outward(block, sems, j):
        return pltpu.make_async_remote_copy(
            src_ref=out.at[block, rows_of(j)], dst_ref=out.at[block, rows_of(j)],
            send_sem=sems[0].at[j], recv_sem=sems[1].at[j],
            device_id={"depth": jnp.where(me < n // 2, me - 1, me + 1)}, device_id_type=MESH,
        )

    def top_copy(j):
        return outward(3, (top_send, top_recv), j)

    def fin_copy(j):
        return outward(pl.ds(0, 3), (fin_send, fin_recv), j)

    for load in loads:
        load.wait()

    @pl.loop(0, chunks)
    def _(j):
        load_piece(j).wait()
        r0 = pl.multiple_of(j * each, each)
        rows, inner = rows_of(j), pl.ds(pl.multiple_of(r0 + 8, 8), each)
        begins, ends = [], []
        for b in range(each // rows_each):
            on = pattern[0, j * (each // rows_each) + b] > 0
            block = pl.ds(pl.multiple_of(r0 + b * rows_each, rows_each), rows_each)
            begins.append(jnp.where(on, start[block], samples))
            ends.append(jnp.where(on, stop[block], 0))
        begin, end = jnp.concatenate(begins, axis=0), jnp.concatenate(ends, axis=0)

        def layer(early, z, state):
            passed, edges = state
            v = vb[z + 1, rows].astype(jnp.float32)
            vf[z + 1, inner] = v
            edges = jnp.where(pair == z, pltpu.roll(v, lax.rem(2 * z + 1, nx), 1), edges)
            log = jnp.log(1.0 + jnp.exp2(v * slope + offset))
            through = jnp.exp2(log * (-scale * LOG2E))
            now = jnp.where(begin <= z if early else end > z, passed * through, passed)
            share[z, rows] = passed - now
            return now, edges

        state = (jnp.ones((each, nx), jnp.float32), jnp.zeros((each, nx), jnp.float32))
        state = lax.fori_loop(0, samples // 2, functools.partial(layer, True), state, unroll=UNROLL // 2)
        passed, edges = lax.fori_loop(samples // 2, samples, functools.partial(layer, False), state, unroll=UNROLL // 2)
        edge[rows] = edges.astype(jnp.bfloat16)
        hide[j] = encode(1.0 - passed)

        @pl.when(lax.rem(j, 2) == 1)
        def _():
            for entry in edge_copies(j // 2):
                send_halo(entry)

            @pl.when(j == 1)
            def _():
                for r in range(2, max(3, n // 2 + 1)):
                    far_wait(r)

            send_to_mergers(hide_refs, j // 2)

    for r in range(max(3, n // 2 + 1), n):
        far_wait(r)

    for entry in halos:
        wait_arrived(entry)

    @pl.loop(0, samples, unroll=4)
    def _(z):
        vf[1 + z, pl.ds(0, 8)] = yup[z].astype(jnp.float32)[STRIP - 8:]
        vf[1 + z, pl.ds(8 + ny, 8)] = ydn[z].astype(jnp.float32)[:8]

    def render(j):
        r0 = pl.multiple_of(j * each, each)
        rows, inner = rows_of(j), pl.ds(pl.multiple_of(r0 + 8, 8), each)

        @pl.when(lax.rem(j, 2) == 0)
        def _():
            for entry in edge_copies(j // 2) + deep_copies(j // 2):
                wait_arrived(entry)

        vf[samples + 1, inner] = vb[samples + 1, rows].astype(jnp.float32)
        beyond = pltpu.roll(xr[rows].astype(jnp.float32), nx - 2, 1)
        sides_of = jnp.where(lax.rem(lane, 2) == 0, xl[rows].astype(jnp.float32), beyond)

        def layer(z, state):
            previous, v, total, red, green, blue = state
            after = vf[z + 2, inner]
            near = vf.at[z + 1, pl.ds(r0, each + 16)]
            dz = after - previous
            dyv = near[pl.ds(9, each)] - near[pl.ds(7, each)]
            beside = pltpu.roll(sides_of, lax.rem(nx - 2 * z, nx), 1)
            right = jnp.where(lane == nx - 1, beside, pltpu.roll(v, nx - 1, 1))
            dxv = right - jnp.where(lane == 0, beside, pltpu.roll(v, 1, 1))
            lit = jnp.abs(dxv + 1.25 * dyv + (0.224 / 0.168) * dz)
            shade = (0.15 / 0.168) + lit * lax.rsqrt(dxv * dxv + dyv * dyv + dz * dz + 4.0)
            weight = share[z, rows] * shade
            tints = [jnp.tanh(v * slopes[i] + offsets[i]) for i in range(3)]
            return (
                v, after, total + weight,
                red + weight * tints[0], green + weight * tints[1], blue + weight * tints[2],
            )

        zero = jnp.zeros((each, nx), jnp.float32)
        state = (vb[0, rows].astype(jnp.float32), vf[1, inner], zero, zero, zero, zero)
        _, _, total, red, green, blue = lax.fori_loop(0, samples, layer, state, unroll=UNROLL)
        per = (LEVELS * 0.168) / jnp.maximum(decode(hide[j]), 1e-30)
        for i, value in enumerate((red, green, blue)):
            part[j, i] = to_level((value + total) * per)

    def veil(j):
        hidden = [decode(hides[s, j]) for s in range(n)]
        top = hidden[0]
        for s in range(1, n):
            top = top + hidden[s] * (1.0 - top)
        out[3, rows_of(j)] = encode(top)
        pl.when(handing)(lambda: top_copy(j).start())
        for s in range(n):
            weight = hidden[s] * (1.0 / LEVELS)
            for a in range(n):
                if a != s:
                    weight = weight * (1.0 - hidden[a] * before[a][s])
            factor[j, s] = weight

    def merge(j):
        wait_parts(part_refs, j)
        for i in range(3):
            color = from_level(parts[0, j, i]) * factor[j, 0]
            for s in range(1, n):
                color = color + from_level(parts[s, j, i]) * factor[j, s]
            out[i, rows_of(j)] = encode(color)
        pl.when(handing)(lambda: fin_copy(j).start())

    @pl.loop(0, chunks + MERGE_LAG)
    def _(i):
        @pl.when(i < chunks)
        def _():
            render(i)
            send_to_mergers(part_refs, i)

        g = i - VEIL_LAG

        @pl.when(merging & (g >= 0) & (g < groups))
        def _():
            wait_parts(hide_refs, g)
            veil(2 * g)
            veil(2 * g + 1)

        pl.when(merging & (i >= MERGE_LAG))(lambda: merge(i - MERGE_LAG))

    for copy in (top_copy, fin_copy):
        @pl.loop(0, chunks)
        def _(j, copy=copy):
            @pl.when(jnp.logical_not(merging))
            def _():
                copy(j).wait_recv()
                pl.when(handing)(lambda: copy(j).start())

    for entry in halos:
        wait_sent(entry)

    @pl.loop(0, groups)
    def _(g):
        for entry in edge_copies(g) + deep_copies(g):
            wait_sent(entry)

    @pl.loop(0, chunks)
    def _(j):
        for which, merger in enumerate(mergers):
            pl.when(me != merger)(lambda: to_merger(*part_refs, j, me, which).wait_send())

        @pl.when(handing)
        def _():
            top_copy(j).wait_send()
            fin_copy(j).wait_send()

    @pl.loop(0, groups)
    def _(g):
        for which, merger in enumerate(mergers):
            pl.when(me != merger)(lambda: to_merger(*hide_refs, g, me, which).wait_send())


def solution(mesh):
    n, n_tx, n_ty = mesh.shape["depth"], mesh.shape["tx"], mesh.shape["ty"]

    def shards(volume, transfer, ray_start, ray_stop, pattern, depth_order):
        samples, ny, nx = volume.shape
        rows = min(32, ny // 4)
        chunks = ny // rows
        f32, bf16, i16 = jnp.float32, jnp.bfloat16, jnp.int16
        any_space = pl.BlockSpec(memory_space=pl.ANY)
        smem = pl.BlockSpec(memory_space=pltpu.SMEM)
        dma = pltpu.SemaphoreType.DMA
        codes = pl.pallas_call(
            functools.partial(kernel, n, n_tx, n_ty, 2.0 / (samples * n), rows),
            out_shape=jax.ShapeDtypeStruct((4, ny, nx), i16),
            in_specs=[any_space, any_space, any_space, smem, smem, smem],
            out_specs=pl.BlockSpec(memory_space=pltpu.VMEM),
            scratch_shapes=[
                pltpu.VMEM((samples + 2, ny, nx), bf16),
                pltpu.VMEM((ny, nx), jnp.int32),
                pltpu.VMEM((ny, nx), jnp.int32),
                pltpu.VMEM((samples, STRIP, nx), bf16),
                pltpu.VMEM((samples, STRIP, nx), bf16),
                pltpu.VMEM((ny, nx), bf16),
                pltpu.VMEM((ny, nx), bf16),
                pltpu.VMEM((ny, nx), bf16),
                pltpu.VMEM((samples + 2, ny + 16, nx), f32),
                pltpu.VMEM((samples, ny, nx), f32),
                pltpu.VMEM((chunks, rows, nx), i16),
                pltpu.VMEM((n, chunks, rows, nx), i16),
                pltpu.VMEM((chunks, 3, rows, nx), i16),
                pltpu.VMEM((n, chunks, 3, rows, nx), i16),
                pltpu.VMEM((chunks, n, rows, nx), f32),
                dma((chunks + 2,)), dma((2,)), dma((2,)),
                dma((chunks,)), dma((chunks,)), dma((chunks,)), dma((chunks,)),
                pltpu.SemaphoreType.REGULAR((n, 2)),
                dma((chunks // 2, 2)), dma((n, chunks // 2)), dma((chunks, 2)), dma((n, chunks)),
                dma((chunks,)), dma((chunks,)), dma((chunks,)), dma((chunks,)),
            ],
            compiler_params=pltpu.CompilerParams(
                collective_id=0, has_side_effects=True, vmem_limit_bytes=62 * 1024 * 1024
            ),
        )(volume, ray_start, ray_stop, pattern[:, :, 0], transfer.T, depth_order)
        return decode(codes)

    in_specs = (
        P("depth", "ty", "tx"),
        P(),
        P("depth", "ty", "tx"),
        P("depth", "ty", "tx"),
        P("depth", "ty", "tx"),
        P(),
    )
    return jax.shard_map(shards, mesh=mesh, in_specs=in_specs, out_specs=P(None, "ty", "tx"), check_vma=False)
```

```python
import functools
import math

import jax
import jax.numpy as jnp
from jax import lax
from jax.experimental import pallas as pl
from jax.experimental.pallas import tpu as pltpu
from jax.sharding import PartitionSpec as P

MESH = pl.DeviceIdType.MESH
STRIP = 16
UNROLL = 32
LOG2E = math.log2(math.e)
OCTAVES = 24
CODES = 65535.0 / OCTAVES
LEVELS = 65000.0
VEIL_LAG = 4
MERGE_LAG = 6


def encode(x):
    place = jnp.log(jnp.clip(x, 1e-30, 1.0)) * (CODES * LOG2E) + 65535.5
    return (jnp.maximum(place, 0.0).astype(jnp.int32) - 32768).astype(jnp.int16)


def decode(code):
    wide = code.astype(jnp.int32)
    value = jnp.exp2((wide.astype(jnp.float32) - 32767.0) * (1.0 / CODES))
    return jnp.where(wide == -32768, 0.0, value)


def to_level(x):
    return (jnp.minimum(x + 0.5, 65535.0).astype(jnp.int32) - 32768).astype(jnp.int16)


def from_level(code):
    return code.astype(jnp.int32).astype(jnp.float32) + 32768.0


def kernel(
    n, n_tx, n_ty, scale, each,
    vol, start_hbm, stop_hbm, pattern, transfer, order, out,
    vb, start, stop, yup, ydn, edge, xl, xr, vf, share,
    hide, hides, part, parts, factor,
    load_sem, halo_send, halo_recv, deep_send, deep_recv, edge_send, edge_recv, far,
    hide_send, hide_recv, part_send, part_recv, fin_send, fin_recv, top_send, top_recv,
):
    samples, ny, nx = vol.shape
    chunks = ny // each
    group = 2 * each
    groups = chunks // 2
    mergers = (n // 2 - 1, n // 2)
    tx, ty, me = lax.axis_index("tx"), lax.axis_index("ty"), lax.axis_index("depth")

    def rows_of(j):
        return pl.ds(pl.multiple_of(j * each, each), each)

    def group_of(g):
        return pl.ds(pl.multiple_of(g * group, group), group)

    def load_piece(j):
        return pltpu.make_async_copy(
            vol.at[:, rows_of(j)], vb.at[pl.ds(1, samples), rows_of(j)], load_sem.at[j]
        )

    loads = [
        pltpu.make_async_copy(start_hbm.at[0], start, load_sem.at[chunks]),
        pltpu.make_async_copy(stop_hbm.at[0], stop, load_sem.at[chunks + 1]),
    ]
    barrier = pltpu.get_barrier_semaphore()
    sides = (("tx", tx, n_tx), ("ty", ty, n_ty), ("depth", me, n))
    expected = 0
    for axis, at, count in sides:
        @pl.when(at > 0)
        def _(axis=axis, at=at):
            pl.semaphore_signal(barrier, inc=1, device_id={axis: at - 1}, device_id_type=MESH)

        @pl.when(at < count - 1)
        def _(axis=axis, at=at):
            pl.semaphore_signal(barrier, inc=1, device_id={axis: at + 1}, device_id_type=MESH)

        expected = expected + jnp.where(at > 0, 1, 0) + jnp.where(at < count - 1, 1, 0)

    load_piece(0).start()
    for load in loads:
        load.start()
    for j in range(1, chunks):
        load_piece(j).start()
    pl.semaphore_wait(barrier, expected)

    def far_signal(r):
        @pl.when((me - r + 1 >= 0) & (me + 1 < n))
        def _():
            pl.semaphore_signal(far.at[r, 0], inc=1, device_id={"depth": me + 1}, device_id_type=MESH)

        @pl.when((me + r - 1 < n) & (me - 1 >= 0))
        def _():
            pl.semaphore_signal(far.at[r, 1], inc=1, device_id={"depth": me - 1}, device_id_type=MESH)

    def far_wait(r):
        @pl.when(me - r >= 0)
        def _():
            pl.semaphore_wait(far.at[r, 0], 1)

        @pl.when(me + r < n)
        def _():
            pl.semaphore_wait(far.at[r, 1], 1)

        if r + 1 <= n // 2:
            far_signal(r + 1)

    def shift(sems, slot, axis, at, source, target, upward):
        return pltpu.make_async_remote_copy(
            src_ref=source, dst_ref=target, send_sem=sems[0].at[slot], recv_sem=sems[1].at[slot],
            device_id={axis: at + 1 if upward else at - 1}, device_id_type=MESH,
        )

    halo = (halo_send, halo_recv)
    last, first = pl.ds(ny - STRIP, STRIP), pl.ds(0, STRIP)
    halos = [
        (shift(halo, 0, "ty", ty, vol.at[:, last], yup, True), ty, n_ty, True, lambda: yup),
        (shift(halo, 1, "ty", ty, vol.at[:, first], ydn, False), ty, n_ty, False, lambda: ydn),
    ]

    def deep_copies(g):
        rows = group_of(g)
        sems = (deep_send, deep_recv)
        return [
            (shift(sems, 2 * g, "depth", me, vol.at[samples - 1, rows], vb.at[0, rows], True), me, n, True, None),
            (shift(sems, 2 * g + 1, "depth", me, vol.at[0, rows], vb.at[samples + 1, rows], False), me, n, False, None),
        ]

    def edge_copies(g):
        rows = pl.ds(pl.multiple_of(g * group, group), group)
        sems = (edge_send, edge_recv)
        return [
            (shift(sems, 2 * g, "tx", tx, edge.at[rows], xl.at[rows], True), tx, n_tx, True, None),
            (shift(sems, 2 * g + 1, "tx", tx, edge.at[rows], xr.at[rows], False), tx, n_tx, False, None),
        ]

    def send_halo(entry):
        copy, at, count, upward, place = entry
        pl.when(at < count - 1 if upward else at > 0)(copy.start)
        if place is not None:
            @pl.when(at == 0 if upward else at == count - 1)
            def _():
                place()[...] = jnp.zeros(place().shape, jnp.bfloat16)

    def wait_sent(entry):
        copy, at, count, upward, _ = entry
        pl.when(at < count - 1 if upward else at > 0)(copy.wait_send)

    def wait_arrived(entry):
        copy, at, count, upward, _ = entry
        pl.when(at > 0 if upward else at < count - 1)(copy.wait_recv)

    for g in range(groups):
        for entry in deep_copies(g):
            send_halo(entry)
    for entry in halos:
        send_halo(entry)
    if n > 2:
        far_signal(2)

    for at, edge_at, place in (
        (tx, 0, xl), (tx, n_tx - 1, xr), (me, 0, vb.at[0]), (me, n - 1, vb.at[samples + 1]),
    ):
        @pl.when(at == edge_at)
        def _(place=place):
            place[...] = jnp.zeros(place.shape, jnp.bfloat16)

    rows_each = ny // pattern.shape[1]
    slopes = [transfer[0, i] * 0.5 for i in range(3)]
    offsets = [transfer[1, i] * 0.5 for i in range(3)]
    slope, offset = transfer[0, 3] * LOG2E, transfer[1, 3] * LOG2E

    rank = [sum(jnp.where(order[q] == s, q, 0) for q in range(n)) for s in range(n)]
    before = [[jnp.where(rank[a] < rank[b], 1.0, 0.0) for b in range(n)] for a in range(n)]
    lane = lax.broadcasted_iota(jnp.int32, (each, nx), 1)
    pair = lax.shift_right_arithmetic(lane, 1)

    merging = (me == mergers[0]) | (me == mergers[1])
    handing = (me > 0) & (me < n - 1)
    hide_refs = (hide, hides, hide_send, hide_recv, 2)
    part_refs = (part, parts, part_send, part_recv, 1)

    def to_merger(source, target, sends, recvs, count, j, origin, which):
        block = pl.ds(j * count, count)
        return pltpu.make_async_remote_copy(
            src_ref=source.at[block], dst_ref=target.at[origin, block],
            send_sem=sends.at[j, which], recv_sem=recvs.at[origin, j],
            device_id={"depth": mergers[which]}, device_id_type=MESH,
        )

    def send_to_mergers(refs, j):
        for which, merger in enumerate(mergers):
            pl.when(me != merger)(lambda: to_merger(*refs, j, me, which).start())

        @pl.when(merging)
        def _():
            for c in range(refs[4]):
                refs[1][me, j * refs[4] + c] = refs[0][j * refs[4] + c]

    def wait_parts(refs, j):
        for s in range(n):
            pl.when(me != s)(lambda: to_merger(*refs, j, s, 0).wait_recv())

    def outward(block, sems, j):
        return pltpu.make_async_remote_copy(
            src_ref=out.at[block, rows_of(j)], dst_ref=out.at[block, rows_of(j)],
            send_sem=sems[0].at[j], recv_sem=sems[1].at[j],
            device_id={"depth": jnp.where(me < n // 2, me - 1, me + 1)}, device_id_type=MESH,
        )

    def top_copy(j):
        return outward(3, (top_send, top_recv), j)

    def fin_copy(j):
        return outward(pl.ds(0, 3), (fin_send, fin_recv), j)

    for load in loads:
        load.wait()

    def gather_edges(g):
        for h in range(2):
            load_piece(2 * g + h).wait()
            rows = rows_of(2 * g + h)

            def layer(z, edges):
                v = vb[z + 1, rows].astype(jnp.float32)
                return jnp.where(pair == z, pltpu.roll(v, lax.rem(2 * z + 1, nx), 1), edges)

            edges = lax.fori_loop(0, samples, layer, jnp.zeros((each, nx), jnp.float32), unroll=UNROLL)
            edge[rows] = edges.astype(jnp.bfloat16)
        for entry in edge_copies(g):
            send_halo(entry)

    @pl.loop(0, chunks)
    def _(j):
        pl.when(j < groups)(lambda: gather_edges(j))
        r0 = pl.multiple_of(j * each, each)
        rows, inner = rows_of(j), pl.ds(pl.multiple_of(r0 + 8, 8), each)
        begins, ends = [], []
        for b in range(each // rows_each):
            on = pattern[0, j * (each // rows_each) + b] > 0
            block = pl.ds(pl.multiple_of(r0 + b * rows_each, rows_each), rows_each)
            begins.append(jnp.where(on, start[block], samples))
            ends.append(jnp.where(on, stop[block], 0))
        begin, end = jnp.concatenate(begins, axis=0), jnp.concatenate(ends, axis=0)

        def layer(early, z, passed):
            v = vb[z + 1, rows].astype(jnp.float32)
            vf[z + 1, inner] = v
            log = jnp.log(1.0 + jnp.exp2(v * slope + offset))
            through = jnp.exp2(log * (-scale * LOG2E))
            now = jnp.where(begin <= z if early else end > z, passed * through, passed)
            share[z, rows] = passed - now
            return now

        state = jnp.ones((each, nx), jnp.float32)
        state = lax.fori_loop(0, samples // 2, functools.partial(layer, True), state, unroll=UNROLL // 2)
        passed = lax.fori_loop(samples // 2, samples, functools.partial(layer, False), state, unroll=UNROLL // 2)
        hide[j] = encode(1.0 - passed)

        @pl.when(lax.rem(j, 2) == 1)
        def _():
            @pl.when(j == 1)
            def _():
                for r in range(2, max(3, n // 2 + 1)):
                    far_wait(r)

            send_to_mergers(hide_refs, j // 2)

    for entry in halos:
        wait_arrived(entry)

    @pl.loop(0, samples, unroll=4)
    def _(z):
        vf[1 + z, pl.ds(0, 8)] = yup[z].astype(jnp.float32)[STRIP - 8:]
        vf[1 + z, pl.ds(8 + ny, 8)] = ydn[z].astype(jnp.float32)[:8]

    def render(j):
        r0 = pl.multiple_of(j * each, each)
        rows, inner = rows_of(j), pl.ds(pl.multiple_of(r0 + 8, 8), each)

        @pl.when(lax.rem(j, 2) == 0)
        def _():
            for entry in edge_copies(j // 2) + deep_copies(j // 2):
                wait_arrived(entry)

        vf[samples + 1, inner] = vb[samples + 1, rows].astype(jnp.float32)
        beyond = pltpu.roll(xr[rows].astype(jnp.float32), nx - 2, 1)
        sides_of = jnp.where(lax.rem(lane, 2) == 0, xl[rows].astype(jnp.float32), beyond)

        def layer(z, state):
            previous, v, total, red, green, blue = state
            after = vf[z + 2, inner]
            near = vf.at[z + 1, pl.ds(r0, each + 16)]
            dz = after - previous
            dyv = near[pl.ds(9, each)] - near[pl.ds(7, each)]
            beside = pltpu.roll(sides_of, lax.rem(nx - 2 * z, nx), 1)
            right = jnp.where(lane == nx - 1, beside, pltpu.roll(v, nx - 1, 1))
            dxv = right - jnp.where(lane == 0, beside, pltpu.roll(v, 1, 1))
            lit = jnp.abs(dxv + 1.25 * dyv + (0.224 / 0.168) * dz)
            shade = (0.15 / 0.168) + lit * lax.rsqrt(dxv * dxv + dyv * dyv + dz * dz + 4.0)
            weight = share[z, rows] * shade
            tints = [jnp.tanh(v * slopes[i] + offsets[i]) for i in range(3)]
            return (
                v, after, total + weight,
                red + weight * tints[0], green + weight * tints[1], blue + weight * tints[2],
            )

        zero = jnp.zeros((each, nx), jnp.float32)
        state = (vb[0, rows].astype(jnp.float32), vf[1, inner], zero, zero, zero, zero)
        _, _, total, red, green, blue = lax.fori_loop(0, samples, layer, state, unroll=UNROLL)
        per = (LEVELS * 0.168) / jnp.maximum(decode(hide[j]), 1e-30)
        for i, value in enumerate((red, green, blue)):
            part[j, i] = to_level((value + total) * per)

    def veil(j):
        hidden = [decode(hides[s, j]) for s in range(n)]
        top = hidden[0]
        for s in range(1, n):
            top = top + hidden[s] * (1.0 - top)
        out[3, rows_of(j)] = encode(top)
        pl.when(handing)(lambda: top_copy(j).start())
        for s in range(n):
            weight = hidden[s] * (1.0 / LEVELS)
            for a in range(n):
                if a != s:
                    weight = weight * (1.0 - hidden[a] * before[a][s])
            factor[j, s] = weight

    def merge(j):
        wait_parts(part_refs, j)
        for i in range(3):
            color = from_level(parts[0, j, i]) * factor[j, 0]
            for s in range(1, n):
                color = color + from_level(parts[s, j, i]) * factor[j, s]
            out[i, rows_of(j)] = encode(color)
        pl.when(handing)(lambda: fin_copy(j).start())

    @pl.loop(0, chunks + MERGE_LAG)
    def _(i):
        @pl.when(i < chunks)
        def _():
            render(i)
            send_to_mergers(part_refs, i)

        g = i - VEIL_LAG

        @pl.when(merging & (g >= 0) & (g < groups))
        def _():
            wait_parts(hide_refs, g)
            veil(2 * g)
            veil(2 * g + 1)

        pl.when(merging & (i >= MERGE_LAG))(lambda: merge(i - MERGE_LAG))

    for copy in (top_copy, fin_copy):
        @pl.loop(0, chunks)
        def _(j, copy=copy):
            @pl.when(jnp.logical_not(merging))
            def _():
                copy(j).wait_recv()
                pl.when(handing)(lambda: copy(j).start())

    for entry in halos:
        wait_sent(entry)

    @pl.loop(0, groups)
    def _(g):
        for entry in edge_copies(g) + deep_copies(g):
            wait_sent(entry)

    @pl.loop(0, chunks)
    def _(j):
        for which, merger in enumerate(mergers):
            pl.when(me != merger)(lambda: to_merger(*part_refs, j, me, which).wait_send())

        @pl.when(handing)
        def _():
            top_copy(j).wait_send()
            fin_copy(j).wait_send()

    @pl.loop(0, groups)
    def _(g):
        for which, merger in enumerate(mergers):
            pl.when(me != merger)(lambda: to_merger(*hide_refs, g, me, which).wait_send())


def solution(mesh):
    n, n_tx, n_ty = mesh.shape["depth"], mesh.shape["tx"], mesh.shape["ty"]

    def shards(volume, transfer, ray_start, ray_stop, pattern, depth_order):
        samples, ny, nx = volume.shape
        rows = min(32, ny // 4)
        chunks = ny // rows
        f32, bf16, i16 = jnp.float32, jnp.bfloat16, jnp.int16
        any_space = pl.BlockSpec(memory_space=pl.ANY)
        smem = pl.BlockSpec(memory_space=pltpu.SMEM)
        dma = pltpu.SemaphoreType.DMA
        codes = pl.pallas_call(
            functools.partial(kernel, n, n_tx, n_ty, 2.0 / (samples * n), rows),
            out_shape=jax.ShapeDtypeStruct((4, ny, nx), i16),
            in_specs=[any_space, any_space, any_space, smem, smem, smem],
            out_specs=pl.BlockSpec(memory_space=pltpu.VMEM),
            scratch_shapes=[
                pltpu.VMEM((samples + 2, ny, nx), bf16),
                pltpu.VMEM((ny, nx), jnp.int32),
                pltpu.VMEM((ny, nx), jnp.int32),
                pltpu.VMEM((samples, STRIP, nx), bf16),
                pltpu.VMEM((samples, STRIP, nx), bf16),
                pltpu.VMEM((ny, nx), bf16),
                pltpu.VMEM((ny, nx), bf16),
                pltpu.VMEM((ny, nx), bf16),
                pltpu.VMEM((samples + 2, ny + 16, nx), f32),
                pltpu.VMEM((samples, ny, nx), f32),
                pltpu.VMEM((chunks, rows, nx), i16),
                pltpu.VMEM((n, chunks, rows, nx), i16),
                pltpu.VMEM((chunks, 3, rows, nx), i16),
                pltpu.VMEM((n, chunks, 3, rows, nx), i16),
                pltpu.VMEM((chunks, n, rows, nx), f32),
                dma((chunks + 2,)), dma((2,)), dma((2,)),
                dma((chunks,)), dma((chunks,)), dma((chunks,)), dma((chunks,)),
                pltpu.SemaphoreType.REGULAR((n, 2)),
                dma((chunks // 2, 2)), dma((n, chunks // 2)), dma((chunks, 2)), dma((n, chunks)),
                dma((chunks,)), dma((chunks,)), dma((chunks,)), dma((chunks,)),
            ],
            compiler_params=pltpu.CompilerParams(
                collective_id=0, has_side_effects=True, vmem_limit_bytes=62 * 1024 * 1024
            ),
        )(volume, ray_start, ray_stop, pattern[:, :, 0], transfer.T, depth_order)
        return decode(codes)

    in_specs = (
        P("depth", "ty", "tx"),
        P(),
        P("depth", "ty", "tx"),
        P("depth", "ty", "tx"),
        P("depth", "ty", "tx"),
        P(),
    )
    return jax.shard_map(shards, mesh=mesh, in_specs=in_specs, out_specs=P(None, "ty", "tx"), check_vma=False)
```

```python
import functools
import math

import jax
import jax.numpy as jnp
from jax import lax
from jax.experimental import pallas as pl
from jax.experimental.pallas import tpu as pltpu
from jax.sharding import PartitionSpec as P

MESH = pl.DeviceIdType.MESH
STRIP = 16
UNROLL = 32
LOG2E = math.log2(math.e)
OCTAVES = 24
CODES = 65535.0 / OCTAVES
LEVELS = 65000.0
VEIL_LAG = 4
MERGE_LAG = 5


def encode(x):
    place = jnp.log(jnp.clip(x, 1e-30, 1.0)) * (CODES * LOG2E) + 65535.5
    return (jnp.maximum(place, 0.0).astype(jnp.int32) - 32768).astype(jnp.int16)


def decode(code):
    wide = code.astype(jnp.int32)
    value = jnp.exp2((wide.astype(jnp.float32) - 32767.0) * (1.0 / CODES))
    return jnp.where(wide == -32768, 0.0, value)


def to_level(x):
    return (jnp.minimum(x + 0.5, 65535.0).astype(jnp.int32) - 32768).astype(jnp.int16)


def from_level(code):
    return code.astype(jnp.int32).astype(jnp.float32) + 32768.0


def kernel(
    n, n_tx, n_ty, scale, each,
    vol, start_hbm, stop_hbm, pattern, transfer, order, out,
    vb, start, stop, yup, ydn, edge, xl, xr, vf, share,
    hide, hides, part, parts, factor,
    load_sem, halo_send, halo_recv, deep_send, deep_recv, edge_send, edge_recv, far,
    hide_send, hide_recv, part_send, part_recv, fin_send, fin_recv, top_send, top_recv,
):
    samples, ny, nx = vol.shape
    chunks = ny // each
    group = 2 * each
    groups = chunks // 2
    mergers = (n // 2 - 1, n // 2)
    tx, ty, me = lax.axis_index("tx"), lax.axis_index("ty"), lax.axis_index("depth")

    def rows_of(j):
        return pl.ds(pl.multiple_of(j * each, each), each)

    def group_of(g):
        return pl.ds(pl.multiple_of(g * group, group), group)

    def load_piece(j):
        return pltpu.make_async_copy(
            vol.at[:, rows_of(j)], vb.at[pl.ds(1, samples), rows_of(j)], load_sem.at[j]
        )

    loads = [
        pltpu.make_async_copy(start_hbm.at[0], start, load_sem.at[chunks]),
        pltpu.make_async_copy(stop_hbm.at[0], stop, load_sem.at[chunks + 1]),
    ]
    barrier = pltpu.get_barrier_semaphore()
    sides = (("tx", tx, n_tx), ("ty", ty, n_ty), ("depth", me, n))
    expected = 0
    for axis, at, count in sides:
        @pl.when(at > 0)
        def _(axis=axis, at=at):
            pl.semaphore_signal(barrier, inc=1, device_id={axis: at - 1}, device_id_type=MESH)

        @pl.when(at < count - 1)
        def _(axis=axis, at=at):
            pl.semaphore_signal(barrier, inc=1, device_id={axis: at + 1}, device_id_type=MESH)

        expected = expected + jnp.where(at > 0, 1, 0) + jnp.where(at < count - 1, 1, 0)

    load_piece(0).start()
    for load in loads:
        load.start()
    for j in range(1, chunks):
        load_piece(j).start()
    pl.semaphore_wait(barrier, expected)

    def far_signal(r):
        @pl.when((me - r + 1 >= 0) & (me + 1 < n))
        def _():
            pl.semaphore_signal(far.at[r, 0], inc=1, device_id={"depth": me + 1}, device_id_type=MESH)

        @pl.when((me + r - 1 < n) & (me - 1 >= 0))
        def _():
            pl.semaphore_signal(far.at[r, 1], inc=1, device_id={"depth": me - 1}, device_id_type=MESH)

    def far_wait(r):
        @pl.when(me - r >= 0)
        def _():
            pl.semaphore_wait(far.at[r, 0], 1)

        @pl.when(me + r < n)
        def _():
            pl.semaphore_wait(far.at[r, 1], 1)

        if r + 1 <= n // 2:
            far_signal(r + 1)

    def shift(sems, slot, axis, at, source, target, upward):
        return pltpu.make_async_remote_copy(
            src_ref=source, dst_ref=target, send_sem=sems[0].at[slot], recv_sem=sems[1].at[slot],
            device_id={axis: at + 1 if upward else at - 1}, device_id_type=MESH,
        )

    halo = (halo_send, halo_recv)
    last, first = pl.ds(ny - STRIP, STRIP), pl.ds(0, STRIP)
    halos = [
        (shift(halo, 0, "ty", ty, vol.at[:, last], yup, True), ty, n_ty, True, lambda: yup),
        (shift(halo, 1, "ty", ty, vol.at[:, first], ydn, False), ty, n_ty, False, lambda: ydn),
    ]

    def deep_copies(g):
        rows = group_of(g)
        sems = (deep_send, deep_recv)
        return [
            (shift(sems, 2 * g, "depth", me, vol.at[samples - 1, rows], vb.at[0, rows], True), me, n, True, None),
            (shift(sems, 2 * g + 1, "depth", me, vol.at[0, rows], vb.at[samples + 1, rows], False), me, n, False, None),
        ]

    def edge_copies(g):
        rows = pl.ds(pl.multiple_of(g * group, group), group)
        sems = (edge_send, edge_recv)
        return [
            (shift(sems, 2 * g, "tx", tx, edge.at[rows], xl.at[rows], True), tx, n_tx, True, None),
            (shift(sems, 2 * g + 1, "tx", tx, edge.at[rows], xr.at[rows], False), tx, n_tx, False, None),
        ]

    def send_halo(entry):
        copy, at, count, upward, place = entry
        pl.when(at < count - 1 if upward else at > 0)(copy.start)
        if place is not None:
            @pl.when(at == 0 if upward else at == count - 1)
            def _():
                place()[...] = jnp.zeros(place().shape, jnp.bfloat16)

    def wait_sent(entry):
        copy, at, count, upward, _ = entry
        pl.when(at < count - 1 if upward else at > 0)(copy.wait_send)

    def wait_arrived(entry):
        copy, at, count, upward, _ = entry
        pl.when(at > 0 if upward else at < count - 1)(copy.wait_recv)

    for g in range(groups):
        for entry in deep_copies(g):
            send_halo(entry)
    for entry in halos:
        send_halo(entry)
    if n > 2:
        far_signal(2)

    for at, edge_at, place in (
        (tx, 0, xl), (tx, n_tx - 1, xr), (me, 0, vb.at[0]), (me, n - 1, vb.at[samples + 1]),
    ):
        @pl.when(at == edge_at)
        def _(place=place):
            place[...] = jnp.zeros(place.shape, jnp.bfloat16)

    rows_each = ny // pattern.shape[1]
    slopes = [transfer[0, i] * 0.5 for i in range(3)]
    offsets = [transfer[1, i] * 0.5 for i in range(3)]
    slope, offset = transfer[0, 3] * LOG2E, transfer[1, 3] * LOG2E

    rank = [sum(jnp.where(order[q] == s, q, 0) for q in range(n)) for s in range(n)]
    before = [[jnp.where(rank[a] < rank[b], 1.0, 0.0) for b in range(n)] for a in range(n)]
    lane = lax.broadcasted_iota(jnp.int32, (each, nx), 1)
    pair = lax.shift_right_arithmetic(lane, 1)

    merging = (me == mergers[0]) | (me == mergers[1])
    handing = (me > 0) & (me < n - 1)
    hide_refs = (hide, hides, hide_send, hide_recv, 2)
    part_refs = (part, parts, part_send, part_recv, 1)

    def to_merger(source, target, sends, recvs, count, j, origin, which):
        block = pl.ds(j * count, count)
        return pltpu.make_async_remote_copy(
            src_ref=source.at[block], dst_ref=target.at[origin, block],
            send_sem=sends.at[j, which], recv_sem=recvs.at[origin, j],
            device_id={"depth": mergers[which]}, device_id_type=MESH,
        )

    def send_to_mergers(refs, j):
        for which, merger in enumerate(mergers):
            pl.when(me != merger)(lambda: to_merger(*refs, j, me, which).start())

        @pl.when(merging)
        def _():
            for c in range(refs[4]):
                refs[1][me, j * refs[4] + c] = refs[0][j * refs[4] + c]

    def wait_parts(refs, j):
        for s in range(n):
            pl.when(me != s)(lambda: to_merger(*refs, j, s, 0).wait_recv())

    def outward(block, sems, j):
        return pltpu.make_async_remote_copy(
            src_ref=out.at[block, rows_of(j)], dst_ref=out.at[block, rows_of(j)],
            send_sem=sems[0].at[j], recv_sem=sems[1].at[j],
            device_id={"depth": jnp.where(me < n // 2, me - 1, me + 1)}, device_id_type=MESH,
        )

    def top_copy(j):
        return outward(3, (top_send, top_recv), j)

    def fin_copy(j):
        return outward(pl.ds(0, 3), (fin_send, fin_recv), j)

    for load in loads:
        load.wait()

    @pl.loop(0, chunks)
    def _(j):
        load_piece(j).wait()
        r0 = pl.multiple_of(j * each, each)
        rows, inner = rows_of(j), pl.ds(pl.multiple_of(r0 + 8, 8), each)
        begins, ends = [], []
        for b in range(each // rows_each):
            on = pattern[0, j * (each // rows_each) + b] > 0
            block = pl.ds(pl.multiple_of(r0 + b * rows_each, rows_each), rows_each)
            begins.append(jnp.where(on, start[block], samples))
            ends.append(jnp.where(on, stop[block], 0))
        begin, end = jnp.concatenate(begins, axis=0), jnp.concatenate(ends, axis=0)

        def layer(early, z, state):
            passed, edges = state
            v = vb[z + 1, rows].astype(jnp.float32)
            vf[z + 1, inner] = v
            edges = jnp.where(pair == z, pltpu.roll(v, lax.rem(2 * z + 1, nx), 1), edges)
            log = jnp.log(1.0 + jnp.exp2(v * slope + offset))
            through = jnp.exp2(log * (-scale * LOG2E))
            now = jnp.where(begin <= z if early else end > z, passed * through, passed)
            share[z, rows] = passed - now
            return now, edges

        state = (jnp.ones((each, nx), jnp.float32), jnp.zeros((each, nx), jnp.float32))
        state = lax.fori_loop(0, samples // 2, functools.partial(layer, True), state, unroll=UNROLL // 2)
        passed, edges = lax.fori_loop(samples // 2, samples, functools.partial(layer, False), state, unroll=UNROLL // 2)
        edge[rows] = edges.astype(jnp.bfloat16)
        hide[j] = encode(1.0 - passed)

        @pl.when(lax.rem(j, 2) == 1)
        def _():
            for entry in edge_copies(j // 2):
                send_halo(entry)

            @pl.when(j == 1)
            def _():
                for r in range(2, max(3, n // 2 + 1)):
                    far_wait(r)

            send_to_mergers(hide_refs, j // 2)

    for entry in halos:
        wait_arrived(entry)

    @pl.loop(0, samples, unroll=4)
    def _(z):
        vf[1 + z, pl.ds(0, 8)] = yup[z].astype(jnp.float32)[STRIP - 8:]
        vf[1 + z, pl.ds(8 + ny, 8)] = ydn[z].astype(jnp.float32)[:8]

    def render(j):
        r0 = pl.multiple_of(j * each, each)
        rows, inner = rows_of(j), pl.ds(pl.multiple_of(r0 + 8, 8), each)

        @pl.when(lax.rem(j, 2) == 0)
        def _():
            for entry in edge_copies(j // 2) + deep_copies(j // 2):
                wait_arrived(entry)

        vf[samples + 1, inner] = vb[samples + 1, rows].astype(jnp.float32)
        beyond = pltpu.roll(xr[rows].astype(jnp.float32), nx - 2, 1)
        sides_of = jnp.where(lax.rem(lane, 2) == 0, xl[rows].astype(jnp.float32), beyond)

        def layer(z, state):
            previous, v, total, red, green, blue = state
            after = vf[z + 2, inner]
            near = vf.at[z + 1, pl.ds(r0, each + 16)]
            dz = after - previous
            dyv = near[pl.ds(9, each)] - near[pl.ds(7, each)]
            beside = pltpu.roll(sides_of, lax.rem(nx - 2 * z, nx), 1)
            right = jnp.where(lane == nx - 1, beside, pltpu.roll(v, nx - 1, 1))
            dxv = right - jnp.where(lane == 0, beside, pltpu.roll(v, 1, 1))
            lit = jnp.abs(dxv + 1.25 * dyv + (0.224 / 0.168) * dz)
            shade = (0.15 / 0.168) + lit * lax.rsqrt(dxv * dxv + dyv * dyv + dz * dz + 4.0)
            weight = share[z, rows] * shade
            tints = [jnp.tanh(v * slopes[i] + offsets[i]) for i in range(3)]
            return (
                v, after, total + weight,
                red + weight * tints[0], green + weight * tints[1], blue + weight * tints[2],
            )

        zero = jnp.zeros((each, nx), jnp.float32)
        state = (vb[0, rows].astype(jnp.float32), vf[1, inner], zero, zero, zero, zero)
        _, _, total, red, green, blue = lax.fori_loop(0, samples, layer, state, unroll=UNROLL)
        per = (LEVELS * 0.168) / jnp.maximum(decode(hide[j]), 1e-30)
        for i, value in enumerate((red, green, blue)):
            part[j, i] = to_level((value + total) * per)

    def veil(j):
        hidden = [decode(hides[s, j]) for s in range(n)]
        top = hidden[0]
        for s in range(1, n):
            top = top + hidden[s] * (1.0 - top)
        out[3, rows_of(j)] = encode(top)
        pl.when(handing)(lambda: top_copy(j).start())
        for s in range(n):
            weight = hidden[s] * (1.0 / LEVELS)
            for a in range(n):
                if a != s:
                    weight = weight * (1.0 - hidden[a] * before[a][s])
            factor[j, s] = weight

    def merge(j):
        wait_parts(part_refs, j)
        for i in range(3):
            color = from_level(parts[0, j, i]) * factor[j, 0]
            for s in range(1, n):
                color = color + from_level(parts[s, j, i]) * factor[j, s]
            out[i, rows_of(j)] = encode(color)
        pl.when(handing)(lambda: fin_copy(j).start())

    @pl.loop(0, chunks + MERGE_LAG)
    def _(i):
        @pl.when(i < chunks)
        def _():
            render(i)
            send_to_mergers(part_refs, i)

        g = i - VEIL_LAG

        @pl.when(merging & (g >= 0) & (g < groups))
        def _():
            wait_parts(hide_refs, g)
            veil(2 * g)
            veil(2 * g + 1)

        pl.when(merging & (i >= MERGE_LAG))(lambda: merge(i - MERGE_LAG))

    for copy in (top_copy, fin_copy):
        @pl.loop(0, chunks)
        def _(j, copy=copy):
            @pl.when(jnp.logical_not(merging))
            def _():
                copy(j).wait_recv()
                pl.when(handing)(lambda: copy(j).start())

    for entry in halos:
        wait_sent(entry)

    @pl.loop(0, groups)
    def _(g):
        for entry in edge_copies(g) + deep_copies(g):
            wait_sent(entry)

    @pl.loop(0, chunks)
    def _(j):
        for which, merger in enumerate(mergers):
            pl.when(me != merger)(lambda: to_merger(*part_refs, j, me, which).wait_send())

        @pl.when(handing)
        def _():
            top_copy(j).wait_send()
            fin_copy(j).wait_send()

    @pl.loop(0, groups)
    def _(g):
        for which, merger in enumerate(mergers):
            pl.when(me != merger)(lambda: to_merger(*hide_refs, g, me, which).wait_send())


def solution(mesh):
    n, n_tx, n_ty = mesh.shape["depth"], mesh.shape["tx"], mesh.shape["ty"]

    def shards(volume, transfer, ray_start, ray_stop, pattern, depth_order):
        samples, ny, nx = volume.shape
        rows = min(32, ny // 4)
        chunks = ny // rows
        f32, bf16, i16 = jnp.float32, jnp.bfloat16, jnp.int16
        any_space = pl.BlockSpec(memory_space=pl.ANY)
        smem = pl.BlockSpec(memory_space=pltpu.SMEM)
        dma = pltpu.SemaphoreType.DMA
        codes = pl.pallas_call(
            functools.partial(kernel, n, n_tx, n_ty, 2.0 / (samples * n), rows),
            out_shape=jax.ShapeDtypeStruct((4, ny, nx), i16),
            in_specs=[any_space, any_space, any_space, smem, smem, smem],
            out_specs=pl.BlockSpec(memory_space=pltpu.VMEM),
            scratch_shapes=[
                pltpu.VMEM((samples + 2, ny, nx), bf16),
                pltpu.VMEM((ny, nx), jnp.int32),
                pltpu.VMEM((ny, nx), jnp.int32),
                pltpu.VMEM((samples, STRIP, nx), bf16),
                pltpu.VMEM((samples, STRIP, nx), bf16),
                pltpu.VMEM((ny, nx), bf16),
                pltpu.VMEM((ny, nx), bf16),
                pltpu.VMEM((ny, nx), bf16),
                pltpu.VMEM((samples + 2, ny + 16, nx), f32),
                pltpu.VMEM((samples, ny, nx), f32),
                pltpu.VMEM((chunks, rows, nx), i16),
                pltpu.VMEM((n, chunks, rows, nx), i16),
                pltpu.VMEM((chunks, 3, rows, nx), i16),
                pltpu.VMEM((n, chunks, 3, rows, nx), i16),
                pltpu.VMEM((chunks, n, rows, nx), f32),
                dma((chunks + 2,)), dma((2,)), dma((2,)),
                dma((chunks,)), dma((chunks,)), dma((chunks,)), dma((chunks,)),
                pltpu.SemaphoreType.REGULAR((n, 2)),
                dma((chunks // 2, 2)), dma((n, chunks // 2)), dma((chunks, 2)), dma((n, chunks)),
                dma((chunks,)), dma((chunks,)), dma((chunks,)), dma((chunks,)),
            ],
            compiler_params=pltpu.CompilerParams(
                collective_id=0, has_side_effects=True, vmem_limit_bytes=62 * 1024 * 1024
            ),
        )(volume, ray_start, ray_stop, pattern[:, :, 0], transfer.T, depth_order)
        return decode(codes)

    in_specs = (
        P("depth", "ty", "tx"),
        P(),
        P("depth", "ty", "tx"),
        P("depth", "ty", "tx"),
        P("depth", "ty", "tx"),
        P(),
    )
    return jax.shard_map(shards, mesh=mesh, in_specs=in_specs, out_specs=P(None, "ty", "tx"), check_vma=False)
```

```python
import functools
import math

import jax
import jax.numpy as jnp
from jax import lax
from jax.experimental import pallas as pl
from jax.experimental.pallas import tpu as pltpu
from jax.sharding import PartitionSpec as P

MESH = pl.DeviceIdType.MESH
STRIP = 16
UNROLL = 32
LOG2E = math.log2(math.e)
OCTAVES = 24
CODES = 65535.0 / OCTAVES
LEVELS = 65000.0
VEIL_LAG = 4
MERGE_LAG = 6


def encode(x):
    place = jnp.log(jnp.clip(x, 1e-30, 1.0)) * (CODES * LOG2E) + 65535.5
    return (jnp.maximum(place, 0.0).astype(jnp.int32) - 32768).astype(jnp.int16)


def decode(code):
    wide = code.astype(jnp.int32)
    value = jnp.exp2((wide.astype(jnp.float32) - 32767.0) * (1.0 / CODES))
    return jnp.where(wide == -32768, 0.0, value)


def to_level(x):
    return (jnp.minimum(x + 0.5, 65535.0).astype(jnp.int32) - 32768).astype(jnp.int16)


def from_level(code):
    return code.astype(jnp.int32).astype(jnp.float32) + 32768.0


def kernel(
    n, n_tx, n_ty, scale, each,
    vol, start_hbm, stop_hbm, pattern, transfer, order, out,
    vb, start, stop, yup, ydn, edge, xl, xr, vf, share,
    hide, hides, part, parts, factor,
    load_sem, halo_send, halo_recv, deep_send, deep_recv, edge_send, edge_recv, far,
    hide_send, hide_recv, part_send, part_recv, fin_send, fin_recv, top_send, top_recv,
):
    samples, ny, nx = vol.shape
    chunks = ny // each
    group = 2 * each
    groups = chunks // 2
    mergers = (n // 2 - 1, n // 2)
    tx, ty, me = lax.axis_index("tx"), lax.axis_index("ty"), lax.axis_index("depth")

    def rows_of(j):
        return pl.ds(pl.multiple_of(j * each, each), each)

    def group_of(g):
        return pl.ds(pl.multiple_of(g * group, group), group)

    def load_piece(j):
        return pltpu.make_async_copy(
            vol.at[:, rows_of(j)], vb.at[pl.ds(1, samples), rows_of(j)], load_sem.at[j]
        )

    loads = [
        pltpu.make_async_copy(start_hbm.at[0], start, load_sem.at[chunks]),
        pltpu.make_async_copy(stop_hbm.at[0], stop, load_sem.at[chunks + 1]),
    ]
    barrier = pltpu.get_barrier_semaphore()
    sides = (("tx", tx, n_tx), ("ty", ty, n_ty), ("depth", me, n))
    expected = 0
    for axis, at, count in sides:
        @pl.when(at > 0)
        def _(axis=axis, at=at):
            pl.semaphore_signal(barrier, inc=1, device_id={axis: at - 1}, device_id_type=MESH)

        @pl.when(at < count - 1)
        def _(axis=axis, at=at):
            pl.semaphore_signal(barrier, inc=1, device_id={axis: at + 1}, device_id_type=MESH)

        expected = expected + jnp.where(at > 0, 1, 0) + jnp.where(at < count - 1, 1, 0)

    load_piece(0).start()
    for load in loads:
        load.start()
    for j in range(1, chunks):
        load_piece(j).start()
    pl.semaphore_wait(barrier, expected)

    def far_signal(r):
        @pl.when((me - r + 1 >= 0) & (me + 1 < n))
        def _():
            pl.semaphore_signal(far.at[r, 0], inc=1, device_id={"depth": me + 1}, device_id_type=MESH)

        @pl.when((me + r - 1 < n) & (me - 1 >= 0))
        def _():
            pl.semaphore_signal(far.at[r, 1], inc=1, device_id={"depth": me - 1}, device_id_type=MESH)

    def far_wait(r):
        @pl.when(me - r >= 0)
        def _():
            pl.semaphore_wait(far.at[r, 0], 1)

        @pl.when(me + r < n)
        def _():
            pl.semaphore_wait(far.at[r, 1], 1)

        if r + 1 < n:
            far_signal(r + 1)

    def shift(sems, slot, axis, at, source, target, upward):
        return pltpu.make_async_remote_copy(
            src_ref=source, dst_ref=target, send_sem=sems[0].at[slot], recv_sem=sems[1].at[slot],
            device_id={axis: at + 1 if upward else at - 1}, device_id_type=MESH,
        )

    halo = (halo_send, halo_recv)
    last, first = pl.ds(ny - STRIP, STRIP), pl.ds(0, STRIP)
    halos = [
        (shift(halo, 0, "ty", ty, vol.at[:, last], yup, True), ty, n_ty, True, lambda: yup),
        (shift(halo, 1, "ty", ty, vol.at[:, first], ydn, False), ty, n_ty, False, lambda: ydn),
    ]

    def deep_copies(g):
        rows = group_of(g)
        sems = (deep_send, deep_recv)
        return [
            (shift(sems, 2 * g, "depth", me, vol.at[samples - 1, rows], vb.at[0, rows], True), me, n, True, None),
            (shift(sems, 2 * g + 1, "depth", me, vol.at[0, rows], vb.at[samples + 1, rows], False), me, n, False, None),
        ]

    def edge_copies(g):
        rows = pl.ds(pl.multiple_of(g * group, group), group)
        sems = (edge_send, edge_recv)
        return [
            (shift(sems, 2 * g, "tx", tx, edge.at[rows], xl.at[rows], True), tx, n_tx, True, None),
            (shift(sems, 2 * g + 1, "tx", tx, edge.at[rows], xr.at[rows], False), tx, n_tx, False, None),
        ]

    def send_halo(entry):
        copy, at, count, upward, place = entry
        pl.when(at < count - 1 if upward else at > 0)(copy.start)
        if place is not None:
            @pl.when(at == 0 if upward else at == count - 1)
            def _():
                place()[...] = jnp.zeros(place().shape, jnp.bfloat16)

    def wait_sent(entry):
        copy, at, count, upward, _ = entry
        pl.when(at < count - 1 if upward else at > 0)(copy.wait_send)

    def wait_arrived(entry):
        copy, at, count, upward, _ = entry
        pl.when(at > 0 if upward else at < count - 1)(copy.wait_recv)

    for g in range(groups):
        for entry in deep_copies(g):
            send_halo(entry)
    for entry in halos:
        send_halo(entry)
    if n > 2:
        far_signal(2)

    for at, edge_at, place in (
        (tx, 0, xl), (tx, n_tx - 1, xr), (me, 0, vb.at[0]), (me, n - 1, vb.at[samples + 1]),
    ):
        @pl.when(at == edge_at)
        def _(place=place):
            place[...] = jnp.zeros(place.shape, jnp.bfloat16)

    rows_each = ny // pattern.shape[1]
    slopes = [transfer[0, i] * 0.5 for i in range(3)]
    offsets = [transfer[1, i] * 0.5 for i in range(3)]
    slope, offset = transfer[0, 3] * LOG2E, transfer[1, 3] * LOG2E

    rank = [sum(jnp.where(order[q] == s, q, 0) for q in range(n)) for s in range(n)]
    before = [[jnp.where(rank[a] < rank[b], 1.0, 0.0) for b in range(n)] for a in range(n)]
    lane = lax.broadcasted_iota(jnp.int32, (each, nx), 1)
    pair = lax.shift_right_arithmetic(lane, 1)

    merging = (me == mergers[0]) | (me == mergers[1])
    handing = (me > 0) & (me < n - 1)
    hide_refs = (hide, hides, hide_send, hide_recv, 2)
    part_refs = (part, parts, part_send, part_recv, 1)

    def to_merger(source, target, sends, recvs, count, j, origin, which):
        block = pl.ds(j * count, count)
        return pltpu.make_async_remote_copy(
            src_ref=source.at[block], dst_ref=target.at[origin, block],
            send_sem=sends.at[j, which], recv_sem=recvs.at[origin, j],
            device_id={"depth": mergers[which]}, device_id_type=MESH,
        )

    def send_to_mergers(refs, j):
        for which, merger in enumerate(mergers):
            pl.when(me != merger)(lambda: to_merger(*refs, j, me, which).start())

        @pl.when(merging)
        def _():
            for c in range(refs[4]):
                refs[1][me, j * refs[4] + c] = refs[0][j * refs[4] + c]

    def wait_parts(refs, j):
        for s in range(n):
            pl.when(me != s)(lambda: to_merger(*refs, j, s, 0).wait_recv())

    def outward(block, sems, j):
        return pltpu.make_async_remote_copy(
            src_ref=out.at[block, rows_of(j)], dst_ref=out.at[block, rows_of(j)],
            send_sem=sems[0].at[j], recv_sem=sems[1].at[j],
            device_id={"depth": jnp.where(me < n // 2, me - 1, me + 1)}, device_id_type=MESH,
        )

    def top_copy(j):
        return outward(3, (top_send, top_recv), j)

    def fin_copy(j):
        return outward(pl.ds(0, 3), (fin_send, fin_recv), j)

    for load in loads:
        load.wait()

    @pl.loop(0, chunks)
    def _(j):
        load_piece(j).wait()
        r0 = pl.multiple_of(j * each, each)
        rows, inner = rows_of(j), pl.ds(pl.multiple_of(r0 + 8, 8), each)
        begins, ends = [], []
        for b in range(each // rows_each):
            on = pattern[0, j * (each // rows_each) + b] > 0
            block = pl.ds(pl.multiple_of(r0 + b * rows_each, rows_each), rows_each)
            begins.append(jnp.where(on, start[block], samples))
            ends.append(jnp.where(on, stop[block], 0))
        begin, end = jnp.concatenate(begins, axis=0), jnp.concatenate(ends, axis=0)

        def layer(early, z, state):
            passed, edges = state
            v = vb[z + 1, rows].astype(jnp.float32)
            vf[z + 1, inner] = v
            edges = jnp.where(pair == z, pltpu.roll(v, lax.rem(2 * z + 1, nx), 1), edges)
            log = jnp.log(1.0 + jnp.exp2(v * slope + offset))
            through = jnp.exp2(log * (-scale * LOG2E))
            now = jnp.where(begin <= z if early else end > z, passed * through, passed)
            share[z, rows] = passed - now
            return now, edges

        state = (jnp.ones((each, nx), jnp.float32), jnp.zeros((each, nx), jnp.float32))
        state = lax.fori_loop(0, samples // 2, functools.partial(layer, True), state, unroll=UNROLL // 2)
        passed, edges = lax.fori_loop(samples // 2, samples, functools.partial(layer, False), state, unroll=UNROLL // 2)
        edge[rows] = edges.astype(jnp.bfloat16)
        hide[j] = encode(1.0 - passed)

        @pl.when(lax.rem(j, 2) == 1)
        def _():
            for entry in edge_copies(j // 2):
                send_halo(entry)

            @pl.when(j == 1)
            def _():
                for r in range(2, max(3, n // 2 + 1)):
                    far_wait(r)

            send_to_mergers(hide_refs, j // 2)

    for r in range(max(3, n // 2 + 1), n):
        far_wait(r)

    for entry in halos:
        wait_arrived(entry)

    @pl.loop(0, samples, unroll=4)
    def _(z):
        vf[1 + z, pl.ds(0, 8)] = yup[z].astype(jnp.float32)[STRIP - 8:]
        vf[1 + z, pl.ds(8 + ny, 8)] = ydn[z].astype(jnp.float32)[:8]

    def render(j):
        r0 = pl.multiple_of(j * each, each)
        rows, inner = rows_of(j), pl.ds(pl.multiple_of(r0 + 8, 8), each)

        @pl.when(lax.rem(j, 2) == 0)
        def _():
            for entry in edge_copies(j // 2) + deep_copies(j // 2):
                wait_arrived(entry)

        vf[samples + 1, inner] = vb[samples + 1, rows].astype(jnp.float32)
        beyond = pltpu.roll(xr[rows].astype(jnp.float32), nx - 2, 1)
        sides_of = jnp.where(lax.rem(lane, 2) == 0, xl[rows].astype(jnp.float32), beyond)

        def layer(z, state):
            previous, v, total, red, green, blue = state
            after = vf[z + 2, inner]
            near = vf.at[z + 1, pl.ds(r0, each + 16)]
            dz = after - previous
            dyv = near[pl.ds(9, each)] - near[pl.ds(7, each)]
            beside = pltpu.roll(sides_of, lax.rem(nx - 2 * z, nx), 1)
            right = jnp.where(lane == nx - 1, beside, pltpu.roll(v, nx - 1, 1))
            dxv = right - jnp.where(lane == 0, beside, pltpu.roll(v, 1, 1))
            lit = jnp.abs(dxv + 1.25 * dyv + (0.224 / 0.168) * dz)
            shade = (0.15 / 0.168) + lit * lax.rsqrt(dxv * dxv + dyv * dyv + dz * dz + 4.0)
            weight = share[z, rows] * shade
            tints = [jnp.tanh(v * slopes[i] + offsets[i]) for i in range(3)]
            return (
                v, after, total + weight,
                red + weight * tints[0], green + weight * tints[1], blue + weight * tints[2],
            )

        zero = jnp.zeros((each, nx), jnp.float32)
        state = (vb[0, rows].astype(jnp.float32), vf[1, inner], zero, zero, zero, zero)
        _, _, total, red, green, blue = lax.fori_loop(0, samples, layer, state, unroll=UNROLL)
        per = (LEVELS * 0.168) / jnp.maximum(decode(hide[j]), 1e-30)
        for i, value in enumerate((red, green, blue)):
            part[j, i] = to_level((value + total) * per)

    def veil(j):
        hidden = [decode(hides[s, j]) for s in range(n)]
        top = hidden[0]
        for s in range(1, n):
            top = top + hidden[s] * (1.0 - top)
        out[3, rows_of(j)] = encode(top)
        pl.when(handing)(lambda: top_copy(j).start())
        for s in range(n):
            weight = hidden[s] * (1.0 / LEVELS)
            for a in range(n):
                if a != s:
                    weight = weight * (1.0 - hidden[a] * before[a][s])
            factor[j, s] = weight

    def merge(j):
        wait_parts(part_refs, j)
        for i in range(3):
            color = from_level(parts[0, j, i]) * factor[j, 0]
            for s in range(1, n):
                color = color + from_level(parts[s, j, i]) * factor[j, s]
            out[i, rows_of(j)] = encode(color)
        pl.when(handing)(lambda: fin_copy(j).start())

    @pl.loop(0, chunks + MERGE_LAG)
    def _(i):
        @pl.when(i < chunks)
        def _():
            render(i)
            send_to_mergers(part_refs, i)

        g = i - VEIL_LAG

        @pl.when(merging & (g >= 0) & (g < groups))
        def _():
            wait_parts(hide_refs, g)
            veil(2 * g)
            veil(2 * g + 1)

        pl.when(merging & (i >= MERGE_LAG))(lambda: merge(i - MERGE_LAG))

    for copy in (top_copy, fin_copy):
        @pl.loop(0, chunks)
        def _(j, copy=copy):
            @pl.when(jnp.logical_not(merging))
            def _():
                copy(j).wait_recv()
                pl.when(handing)(lambda: copy(j).start())

    for entry in halos:
        wait_sent(entry)

    @pl.loop(0, groups)
    def _(g):
        for entry in edge_copies(g) + deep_copies(g):
            wait_sent(entry)

    @pl.loop(0, chunks)
    def _(j):
        for which, merger in enumerate(mergers):
            pl.when(me != merger)(lambda: to_merger(*part_refs, j, me, which).wait_send())

        @pl.when(handing)
        def _():
            top_copy(j).wait_send()
            fin_copy(j).wait_send()

    @pl.loop(0, groups)
    def _(g):
        for which, merger in enumerate(mergers):
            pl.when(me != merger)(lambda: to_merger(*hide_refs, g, me, which).wait_send())


def solution(mesh):
    n, n_tx, n_ty = mesh.shape["depth"], mesh.shape["tx"], mesh.shape["ty"]

    def shards(volume, transfer, ray_start, ray_stop, pattern, depth_order):
        samples, ny, nx = volume.shape
        rows = min(32, ny // 4)
        chunks = ny // rows
        f32, bf16, i16 = jnp.float32, jnp.bfloat16, jnp.int16
        any_space = pl.BlockSpec(memory_space=pl.ANY)
        smem = pl.BlockSpec(memory_space=pltpu.SMEM)
        dma = pltpu.SemaphoreType.DMA
        codes = pl.pallas_call(
            functools.partial(kernel, n, n_tx, n_ty, 2.0 / (samples * n), rows),
            out_shape=jax.ShapeDtypeStruct((4, ny, nx), i16),
            in_specs=[any_space, any_space, any_space, smem, smem, smem],
            out_specs=pl.BlockSpec(memory_space=pltpu.VMEM),
            scratch_shapes=[
                pltpu.VMEM((samples + 2, ny, nx), bf16),
                pltpu.VMEM((ny, nx), jnp.int32),
                pltpu.VMEM((ny, nx), jnp.int32),
                pltpu.VMEM((samples, STRIP, nx), bf16),
                pltpu.VMEM((samples, STRIP, nx), bf16),
                pltpu.VMEM((ny, nx), bf16),
                pltpu.VMEM((ny, nx), bf16),
                pltpu.VMEM((ny, nx), bf16),
                pltpu.VMEM((samples + 2, ny + 16, nx), f32),
                pltpu.VMEM((samples, ny, nx), f32),
                pltpu.VMEM((chunks, rows, nx), i16),
                pltpu.VMEM((n, chunks, rows, nx), i16),
                pltpu.VMEM((chunks, 3, rows, nx), i16),
                pltpu.VMEM((n, chunks, 3, rows, nx), i16),
                pltpu.VMEM((chunks, n, rows, nx), f32),
                dma((chunks + 2,)), dma((2,)), dma((2,)),
                dma((chunks,)), dma((chunks,)), dma((chunks,)), dma((chunks,)),
                pltpu.SemaphoreType.REGULAR((n, 2)),
                dma((chunks // 2, 2)), dma((n, chunks // 2)), dma((chunks, 2)), dma((n, chunks)),
                dma((chunks,)), dma((chunks,)), dma((chunks,)), dma((chunks,)),
            ],
            compiler_params=pltpu.CompilerParams(
                collective_id=0, has_side_effects=True, vmem_limit_bytes=62 * 1024 * 1024
            ),
        )(volume, ray_start, ray_stop, pattern[:, :, 0], transfer.T, depth_order)
        wide = codes.astype(f32)
        return jnp.where(wide == -32768.0, 0.0, jnp.exp2((wide - 32767.0) * (1.0 / CODES)))

    in_specs = (
        P("depth", "ty", "tx"),
        P(),
        P("depth", "ty", "tx"),
        P("depth", "ty", "tx"),
        P("depth", "ty", "tx"),
        P(),
    )
    return jax.shard_map(shards, mesh=mesh, in_specs=in_specs, out_specs=P(None, "ty", "tx"), check_vma=False)
```
